32 devices in a mesh: dp: 8 (over z, x), row: 2 (over y), col: 2 (over core).
Axes of the slice: x: 2, y: 2, z: 4, core: 2. Of those that a mesh axis runs over, the one named last changes fastest.
Arguments:
- block_input: float32 [4096, 640], P(('dp', 'col'), 'row'), may hold values from -200 to 200
- segment_ids: int32 [16, 256], P(('dp', 'row')), may hold values from 0 to 3, never falling along the last dimension, each value on 1 to 128 neighbouring positions
- w_query: bfloat16 [640, 1024], P('row', 'col'), may hold values from -0.25 to 0.25
- w_key: bfloat16 [640, 256], P('row'), may hold values from -0.25 to 0.25
- w_value: bfloat16 [640, 256], P('row'), may hold values from -0.25 to 0.25
- w_out: bfloat16 [1024, 640], P('col', 'row'), may hold values from -0.1875 to 0.1875
- w_gate: bfloat16 [640, 2048], P('row', 'col'), may hold values from -0.25 to 0.25
- w_up: bfloat16 [640, 2048], P('row', 'col'), may hold values from -0.25 to 0.25
- w_down: bfloat16 [2048, 640], P('col', 'row'), may hold values from -0.125 to 0.125
- gain_input: float32 [640], P('row'), may hold values from 0.25 to 1.75
- gain_attn: float32 [640], P('row'), may hold values from 0.25 to 1.75
- gain_ffn_pre: float32 [640], P('row'), may hold values from 0.25 to 1.75
- gain_ffn_post: float32 [640], P('row'), may hold values from 0.25 to 1.75
- gain_query: float32 [256], replicated, may hold values from 0.25 to 1.75
- gain_key: float32 [256], replicated, may hold values from 0.25 to 1.75
- out_cotangent: float32 [4096, 640], P(('dp', 'col'), 'row'), may hold values from -6 to 6
Outputs:
- block_output: float32 [4096, 640], P(('dp', 'col'), 'row')
- input_grad: float32 [4096, 640], P(('dp', 'col'), 'row')
- query_grad: float32 [640, 1024], P('row', 'col')
- key_grad: float32 [640, 256], P('row')
- value_grad: float32 [640, 256], P('row')
- out_grad: float32 [1024, 640], P('col', 'row')
- gate_grad: float32 [640, 2048], P('row', 'col')
- up_grad: float32 [640, 2048], P('row', 'col')
- down_grad: float32 [2048, 640], P('col', 'row')
- gain_input_grad: float32 [640], P('row')
- gain_attn_grad: float32 [640], P('row')
- gain_ffn_pre_grad: float32 [640], P('row')
- gain_ffn_post_grad: float32 [640], P('row')
- gain_query_grad: float32 [256], replicated
- gain_key_grad: float32 [256], replicated
The draws below stay inside these ranges and needn't reach their ends.
Inputs may be any that keep to these rules, and one draw needn't show every extreme that they name: `segment_ids`: one packed sequence a row; document numbers never fall, start at 0 and take every value up to 3; each document has 1 to 128 tokens and one has exactly 128.
All inputs are finite; a program needn't handle non-finite values.
Results may differ from the reference program's by a relative error of at most 0.014.
Values may be sent and summed in bfloat16 or wider, within the bound.
No kernel may reach another device: no remote copies, remote signals or barrier semaphores. Data moves between devices by JAX's collectives and lax.ppermute only.
A program may use at most 64 MiB of HBM per device.

```python
import math
import jax
import jax.numpy as jnp
import numpy as np
from jax import lax

D = 640
FF = 2048
HQ = 4
HD = 256
SEQ_LEN = 256
SEQS = 16
TOKENS = 4096
DOCS = 4
DOC_MOST = 128
N_COL = 2


def draw_block_input(key, part):
    key_noise, key_rows, key_cols = jax.random.split(key, 3)
    columns = jnp.arange(D, dtype=jnp.float32) / D
    col_scale = jnp.exp(jax.random.uniform(key_cols, (1, D), jnp.float32, 0.0, 2.3) + 1.1 * columns)
    noise_draw = jax.random.normal(key_noise, (TOKENS, D), jnp.float32)
    row_scale = jnp.exp(jax.random.uniform(key_rows, (TOKENS, 1), jnp.float32, 0.0, 2.3))
    return jnp.clip(noise_draw * row_scale * col_scale / 15.0, -200.0, 200.0)


def shard_levels(own_key, dims, cuts, least, top_value):
    level = 1.0
    for position, shards_of in cuts:
        heights = jax.random.uniform(jax.random.fold_in(jax.random.fold_in(own_key, 6), position), (shards_of,), jnp.float32, least / len(cuts), top_value / len(cuts))
        level = level * jnp.repeat(jnp.exp(heights), dims[position] // shards_of).reshape((-1,) + (1,) * (len(dims) - 1 - position))
    return level


def length_profile(count, total, reach, lean):
    loads = [(1 << 20) // math.isqrt(standing ** lean) + 1 for standing in range(2, count + 1)]
    spare, given = total - reach - (count - 1), [1] * (count - 1)
    while spare > 0:
        free = [i for i in range(count - 1) if given[i] < reach]
        whole, budget = sum([loads[i] for i in free]), spare
        for i in free:
            extra = min(reach - given[i], max(1, budget * loads[i] // whole), spare)
            given[i] = given[i] + extra
            spare = spare - extra
    return np.array([reach] + given)


def uneven(rng, count, total, reach, slope):
    if count == 2:
        one = jax.random.randint(rng, (), max(1, total - reach), min(reach, total - 1) + 1)
        return jnp.stack([one, total - one])
    sizes = jnp.asarray(length_profile(count, total, reach, slope), jnp.int32)
    pairs = (count - 1) // 2
    source_of, sink = sizes[1:1 + 2 * pairs:2], sizes[2:2 + 2 * pairs:2]
    room = jnp.minimum(source_of - 1, reach - sink)
    shifted = jax.random.randint(jax.random.fold_in(rng, 1), (pairs,), 0, 1 << 20) % (room + 1)
    sizes = sizes.at[1:1 + 2 * pairs:2].set(source_of - shifted).at[2:2 + 2 * pairs:2].set(sink + shifted)
    return sizes[jax.random.permutation(jax.random.fold_in(rng, 2), count)]


def scatter_about(key, extent, deviation, limit, pieces=(), kind=jnp.bfloat16):
    result = deviation * jax.random.normal(key, extent, jnp.float32)
    if pieces:
        result = result * shard_levels(key, extent, pieces, -0.22, 0.18)
    return jnp.clip(result, -limit, limit).astype(kind)


def setup_inputs(seed: int = 0) -> dict:
    key_of = jax.random.split(jax.random.key(seed), 17)
    return {
        "block_input": draw_block_input(jax.random.fold_in(key_of[16], 71), 0),
        "segment_ids": jax.vmap(lambda own: jnp.searchsorted(jnp.cumsum(uneven(own, DOCS, SEQ_LEN, DOC_MOST, 2)), jnp.arange(SEQ_LEN), side="right"))(jax.random.split(key_of[1], SEQS)).reshape((SEQS, SEQ_LEN)).astype(jnp.int32),
        "w_query": scatter_about(key_of[2], (D, HQ * HD), D ** -0.5, 0.25, ((0, 2), (1, 2))),
        "w_key": scatter_about(key_of[3], (D, HD), D ** -0.5, 0.25, ((0, 2),)),
        "w_value": scatter_about(key_of[4], (D, HD), D ** -0.5, 0.25, ((0, 2),)),
        "w_out": scatter_about(key_of[5], (HQ * HD, D), (HQ * HD) ** -0.5, 0.1875, ((0, 2), (1, 2))),
        "w_gate": scatter_about(key_of[6], (D, FF), D ** -0.5, 0.25, ((0, 2), (1, 2))),
        "w_up": scatter_about(key_of[7], (D, FF), D ** -0.5, 0.25, ((0, 2), (1, 2))),
        "w_down": scatter_about(key_of[8], (FF, D), FF ** -0.5, 0.125, ((0, 2), (1, 2))),
        "gain_input": jnp.clip(1.0 + 0.15 * jax.random.normal(key_of[9], (D,), jnp.float32), 0.25, 1.75),
        "gain_attn": jnp.clip(1.0 + 0.15 * jax.random.normal(key_of[10], (D,), jnp.float32), 0.25, 1.75),
        "gain_ffn_pre": jnp.clip(1.0 + 0.15 * jax.random.normal(key_of[11], (D,), jnp.float32), 0.25, 1.75),
        "gain_ffn_post": jnp.clip(1.0 + 0.15 * jax.random.normal(key_of[12], (D,), jnp.float32), 0.25, 1.75),
        "gain_query": jnp.clip(1.0 + 0.15 * jax.random.normal(key_of[13], (HD,), jnp.float32), 0.25, 1.75),
        "gain_key": jnp.clip(1.0 + 0.15 * jax.random.normal(key_of[14], (HD,), jnp.float32), 0.25, 1.75),
        "out_cotangent": scatter_about(key_of[15], (TOKENS, D), 1.0, 6.0, ((0, 16), (1, 2)), jnp.float32),
    }


eps_norm = 1e-06
rope_base = 1000000.0

def rms_scale(values):
    return lax.rsqrt(lax.optimization_barrier(jnp.mean(values * values, axis=-1, keepdims=True)) + eps_norm)

def norm_backward(upstream, values, inv_rms, gain_vector):
    weighted = upstream * gain_vector
    width_sum = lax.optimization_barrier(jnp.sum(weighted * values, axis=-1, keepdims=True))
    through = inv_rms * weighted - values * inv_rms ** 3 * width_sum / values.shape[-1]
    return (through, lax.optimization_barrier(jnp.sum(upstream * values * inv_rms, axis=0)))

def rope_tables(segments):
    length = segments.shape[-1]
    places = jnp.arange(length, dtype=jnp.int32)
    earlier = jnp.concatenate([segments[..., :1] - 1, segments[..., :-1]], axis=-1)
    starts = lax.cummax(jnp.where(segments != earlier, places, 0), axis=segments.ndim - 1)
    offsets = (places - starts).astype(jnp.float32)
    frequency = rope_base ** (-(jnp.arange(HD // 2, dtype=jnp.float32) * 2.0 / HD))
    angles = offsets[..., None] * frequency
    return (jnp.cos(angles), jnp.sin(angles))

def rotate(values, cosine_table, sine_table):
    lower_half = values[..., :HD // 2]
    upper_half = values[..., HD // 2:]
    return jnp.concatenate([lower_half * cosine_table - upper_half * sine_table, upper_half * cosine_table + lower_half * sine_table], axis=-1)

def gelu_tanh(values):
    return jax.nn.gelu(values, approximate=True)

def dense(left, right):
    return jnp.dot(left, right, preferred_element_type=jnp.float32)

def rounded(values):
    return lax.optimization_barrier(values.astype(jnp.bfloat16)).astype(jnp.float32)

def reference(block_input, segment_ids, w_query, w_key, w_value, w_out, w_gate, w_up, w_down, gain_input, gain_attn, gain_ffn_pre, gain_ffn_post, gain_query, gain_key, out_cotangent):
    seq_group = 8
    block_count = SEQS // seq_group
    block_rows = seq_group * SEQ_LEN
    logit_scale_factor = HD ** (-0.5)
    inputs_all = block_input.reshape(block_count, block_rows, D)
    cotangent_all = out_cotangent.reshape(block_count, block_rows, D)
    segments_all = segment_ids.reshape(block_count, seq_group, SEQ_LEN)
    half_heads = HQ // N_COL

    def one_block(totals, operands):
        inputs, segments, cotangent = operands
        scale_in = rms_scale(inputs)
        normed_bf = (inputs * scale_in * gain_input).astype(jnp.bfloat16)
        raw_query = dense(normed_bf, w_query).reshape(seq_group, SEQ_LEN, HQ, HD)
        raw_key = dense(normed_bf, w_key).reshape(seq_group, SEQ_LEN, HD)
        raw_value = dense(normed_bf, w_value).reshape(seq_group, SEQ_LEN, HD)
        cosine_table, sine_table = rope_tables(segments)

        def query_map(unnormed, gain_vector):
            return rotate(unnormed * rms_scale(unnormed) * gain_vector, cosine_table[:, :, None, :], sine_table[:, :, None, :])

        def key_map(unnormed, gain_vector):
            return rotate(unnormed * rms_scale(unnormed) * gain_vector, cosine_table, sine_table)
        query_float = rounded(query_map(raw_query, gain_query))
        key_float = rounded(key_map(raw_key, gain_key))
        value_bf = raw_value.astype(jnp.bfloat16)
        value_float = value_bf.astype(jnp.float32)
        places = jnp.arange(SEQ_LEN, dtype=jnp.int32)
        allowed = (segments[:, :, None] == segments[:, None, :]) & (places[None, :, None] >= places[None, None, :])
        allowed = allowed[:, None, :, :]
        attention_logits = jnp.einsum('pljr,per->pjle', query_float, key_float) * logit_scale_factor
        weights = jnp.where(allowed, jnp.exp(attention_logits), 0.0)
        row_total = lax.optimization_barrier(jnp.sum(weights, axis=-1, keepdims=True))
        log_total = jnp.log(row_total)
        probability_float = rounded(weights / row_total)
        mixed_head_outputs = jnp.einsum('girv,gvx->grix', probability_float, value_float)
        heads_bf = mixed_head_outputs.reshape(block_rows, HQ * HD).astype(jnp.bfloat16)
        attn_proj = dense(heads_bf, w_out)
        scale_y = rms_scale(attn_proj)
        resid_mid = inputs + attn_proj * scale_y * gain_attn
        scale_mid = rms_scale(resid_mid)
        ffn_bf = (resid_mid * scale_mid * gain_ffn_pre).astype(jnp.bfloat16)
        gate_value = dense(ffn_bf, w_gate)
        up_value = dense(ffn_bf, w_up)
        gelu_value, gelu_pull = jax.vjp(gelu_tanh, gate_value)
        hidden_bf = (gelu_value * up_value).astype(jnp.bfloat16)
        ffn_out = dense(hidden_bf, w_down)
        scale_f = rms_scale(ffn_out)
        block_out = resid_mid + ffn_out * scale_f * gain_ffn_post
        grad_ffn, post_part = norm_backward(cotangent, ffn_out, scale_f, gain_ffn_post)
        grad_ffn_bf = grad_ffn.astype(jnp.bfloat16)
        down_term = dense(hidden_bf.T, grad_ffn_bf)
        grad_hidden = dense(grad_ffn_bf, w_down.T)
        grad_gate_bf = gelu_pull(grad_hidden * up_value)[0].astype(jnp.bfloat16)
        grad_up_bf = (grad_hidden * gelu_value).astype(jnp.bfloat16)
        gate_term = dense(ffn_bf.T, grad_gate_bf)
        up_term = dense(ffn_bf.T, grad_up_bf)
        grad_pre = dense(grad_gate_bf, w_gate.T) + dense(grad_up_bf, w_up.T)
        grad_mid_norm, pre_part = norm_backward(grad_pre, resid_mid, scale_mid, gain_ffn_pre)
        grad_mid = cotangent + grad_mid_norm
        grad_attn, attn_part = norm_backward(grad_mid, attn_proj, scale_y, gain_attn)
        grad_attn_bf = grad_attn.astype(jnp.bfloat16)
        out_term = dense(heads_bf.T, grad_attn_bf)
        head_gradient_float = rounded(dense(grad_attn_bf, w_out.T)).reshape(seq_group, SEQ_LEN, HQ, HD)
        probs_back = jnp.where(allowed, jnp.exp(attention_logits - log_total), 0.0)
        probs_back_f = rounded(probs_back)
        value_terms = jnp.einsum('bhqk,bqhd->bhkd', probs_back_f, head_gradient_float)
        probability_gradient = jnp.einsum('pljr,per->pjle', head_gradient_float, value_float)
        row_delta = lax.optimization_barrier(jnp.sum(probs_back * probability_gradient, axis=-1, keepdims=True))
        score_gradient = rounded(probs_back * (probability_gradient - row_delta))
        rotated_query_gradient = jnp.einsum('girv,gvx->grix', score_gradient, key_float) * logit_scale_factor
        key_terms = jnp.einsum('bhqk,bqhd->bhkd', score_gradient, query_float) * logit_scale_factor
        half_shape = (seq_group, N_COL, half_heads, SEQ_LEN, HD)
        key_halves = lax.optimization_barrier(jnp.sum(key_terms.reshape(half_shape), axis=2))
        value_halves = lax.optimization_barrier(jnp.sum(value_terms.reshape(half_shape), axis=2))
        query_pull = jax.vjp(query_map, raw_query, gain_query)[1]
        grad_raw_query, query_gain_part = query_pull(rotated_query_gradient)
        key_pull = jax.vjp(key_map, raw_key, gain_key)[1]
        query_grad_bf = grad_raw_query.reshape(block_rows, HQ * HD).astype(jnp.bfloat16)
        grad_in = dense(query_grad_bf, w_query.T)
        query_term = dense(normed_bf.T, query_grad_bf)
        key_term = jnp.zeros((D, HD), jnp.float32)
        value_term = jnp.zeros((D, HD), jnp.float32)
        key_gain_part = jnp.zeros((HD,), jnp.float32)
        for member in range(N_COL):
            grad_raw_key, gain_piece = key_pull(key_halves[:, member])
            key_gain_part = key_gain_part + gain_piece
            key_half_bf = grad_raw_key.reshape(block_rows, HD).astype(jnp.bfloat16)
            value_half_bf = value_halves[:, member].reshape(block_rows, HD).astype(jnp.bfloat16)
            grad_in = grad_in + dense(key_half_bf, w_key.T) + dense(value_half_bf, w_value.T)
            key_term = key_term + dense(normed_bf.T, key_half_bf)
            value_term = value_term + dense(normed_bf.T, value_half_bf)
        grad_x_norm, input_part = norm_backward(grad_in, inputs, scale_in, gain_input)
        input_grad = grad_mid + grad_x_norm
        updates = (query_term, key_term, value_term, out_term, gate_term, up_term, down_term, input_part, attn_part, pre_part, post_part, query_gain_part, key_gain_part)
        totals = tuple((total_item + update_item for total_item, update_item in zip(totals, updates)))
        return (totals, (block_out, input_grad))
    initial = (jnp.zeros((D, HQ * HD), jnp.float32), jnp.zeros((D, HD), jnp.float32), jnp.zeros((D, HD), jnp.float32), jnp.zeros((HQ * HD, D), jnp.float32), jnp.zeros((D, FF), jnp.float32), jnp.zeros((D, FF), jnp.float32), jnp.zeros((FF, D), jnp.float32), jnp.zeros((D,), jnp.float32), jnp.zeros((D,), jnp.float32), jnp.zeros((D,), jnp.float32), jnp.zeros((D,), jnp.float32), jnp.zeros((HD,), jnp.float32), jnp.zeros((HD,), jnp.float32))
    totals, outputs = lax.scan(one_block, initial, (inputs_all, segments_all, cotangent_all))
    block_output = outputs[0].reshape(TOKENS, D)
    input_grad = outputs[1].reshape(TOKENS, D)
    return (block_output, input_grad, totals[0], totals[1], totals[2], totals[3], totals[4], totals[5], totals[6], totals[7], totals[8], totals[9], totals[10], totals[11], totals[12])
```

```python
import jax
import jax.numpy as jnp
from jax import lax
from jax.sharding import PartitionSpec as P

eps_norm = 1e-06
rope_base = 1000000.0
bf16 = jnp.bfloat16
f32 = jnp.float32


def rms_scale(values):
    return lax.rsqrt(jnp.mean(values * values, axis=-1, keepdims=True) + eps_norm)


def norm_back(upstream, values, inv_rms, gain_vector):
    weighted = upstream * gain_vector
    width_sum = jnp.sum(weighted * values, axis=1, keepdims=True)
    through = inv_rms * weighted - values * inv_rms**3 * width_sum / values.shape[1]
    return through, jnp.sum(upstream * values * inv_rms, axis=0)


def rotate(values, cosine_table, sine_table):
    half = values.shape[-1] // 2
    lower_half = values[..., :half]
    upper_half = values[..., half:]
    return jnp.concatenate(
        [
            lower_half * cosine_table - upper_half * sine_table,
            upper_half * cosine_table + lower_half * sine_table,
        ],
        axis=-1,
    )


def gelu_tanh(values):
    return jax.nn.gelu(values, approximate=True)


def dot(left, right, contract=((1,), (0,))):
    return lax.dot_general(left, right, (contract, ((), ())), preferred_element_type=f32)


def make_step(mesh):
    n_dp, n_row, n_col = mesh.shape["dp"], mesh.shape["row"], mesh.shape["col"]
    assert n_row == 2 and n_col == 2
    bits = []
    while (1 << len(bits)) < n_dp:
        bits.append(1 << len(bits))
    assert (1 << len(bits)) == n_dp

    def swap_row(v):
        return lax.ppermute(v, "row", [(0, 1), (1, 0)])

    def swap_col(v):
        return lax.ppermute(v, "col", [(0, 1), (1, 0)])

    def swap_dp(v, bit):
        return lax.ppermute(v, "dp", [(i, i ^ bit) for i in range(n_dp)])

    def off_to_diag(v):
        return lax.ppermute(v, ("row", "col"), [(1, 3), (2, 0)])

    def diag_to_off_col(v):
        return lax.ppermute(v, ("row", "col"), [(0, 1), (3, 2)])

    def diag_to_off_row(v):
        return lax.ppermute(v, ("row", "col"), [(0, 2), (3, 1)])

    def step(
        block_input, segment_ids, w_query, w_key, w_value, w_out, w_gate, w_up, w_down,
        gain_input, gain_attn, gain_ffn_pre, gain_ffn_post, gain_query, gain_key, out_cotangent,
    ):
        seq_rows, half_width = block_input.shape
        width = 2 * half_width
        head_size = w_key.shape[1]
        query_width = w_query.shape[1]
        head_count = query_width // head_size
        hidden_width = w_gate.shape[1]
        scale_factor = head_size ** (-0.5)
        row = lax.axis_index("row")
        col = lax.axis_index("col")
        dp = lax.axis_index("dp")
        diag = row == col
        first_col = col == 0

        def bit_of(bit):
            return (dp // bit) % 2

        def chip_sequence(local):
            other_diag = off_to_diag(local)
            own = jnp.where(diag, local, diag_to_off_col(local))
            other = jnp.where(diag, other_diag, diag_to_off_col(other_diag))
            return jnp.concatenate([own, other], axis=1)

        def other_rows_via(own):
            rows = own.shape[0]
            if n_dp == 1:
                return swap_row(own)
            pieces = own.reshape(2, rows // 2, own.shape[1])
            b = bit_of(1)
            part = lax.dynamic_index_in_dim(pieces, b, 0, keepdims=False)
            mine = swap_row(part)
            theirs = swap_dp(mine, 1)
            return jnp.concatenate(
                [jnp.where(b == 0, mine, theirs), jnp.where(b == 0, theirs, mine)], axis=0
            )

        x = chip_sequence(block_input)
        gains_own = jnp.stack([gain_input, gain_attn, gain_ffn_pre, gain_ffn_post])
        gains = jnp.concatenate([gains_own, swap_row(gains_own)], axis=1)
        g_in, g_attn, g_pre, g_post = (gains[i] for i in range(4))
        joint_own = jnp.concatenate([w_query, jnp.where(first_col, w_key, w_value)], axis=1)
        w_joint = jnp.concatenate([joint_own, swap_row(joint_own)], axis=0)
        out_own = w_out.T
        w_out_t = jnp.concatenate([out_own, swap_row(out_own)], axis=0)
        mix_own = jnp.concatenate([w_gate, w_up], axis=1)
        w_mix = jnp.concatenate([mix_own, other_rows_via(mix_own)], axis=0)
        down_own = w_down.T
        w_down_t = jnp.concatenate([down_own, other_rows_via(down_own)], axis=0)
        cotangent = chip_sequence(out_cotangent)

        segments = segment_ids[0]
        places = jnp.arange(seq_rows, dtype=jnp.int32)
        allowed = (segments[:, None] == segments[None, :]) & (places[:, None] >= places[None, :])
        offsets = jnp.sum(allowed.astype(f32), axis=1) - 1.0
        frequency = rope_base ** (-(jnp.arange(head_size // 2, dtype=f32) * 2.0 / head_size))
        angles = offsets[:, None] * frequency
        cosine_table, sine_table = jnp.cos(angles), jnp.sin(angles)

        def query_map(unnormed, gain_vector):
            return rotate(
                unnormed * rms_scale(unnormed) * gain_vector,
                cosine_table[:, None, :],
                sine_table[:, None, :],
            )

        def key_map(unnormed, gain_vector):
            return rotate(unnormed * rms_scale(unnormed) * gain_vector, cosine_table, sine_table)

        scale_in = rms_scale(x)
        normed = (x * scale_in * g_in).astype(bf16)
        projected = dot(normed, w_joint)
        raw_query = projected[:, :query_width].reshape(seq_rows, head_count, head_size)
        kv_mine = projected[:, query_width:]
        kv_theirs = swap_col(kv_mine)
        raw_key = jnp.where(first_col, kv_mine, kv_theirs)
        raw_value = jnp.where(first_col, kv_theirs, kv_mine)
        query = query_map(raw_query, gain_query).astype(bf16)
        key = key_map(raw_key, gain_key).astype(bf16)
        value = raw_value.astype(bf16)
        logits = jnp.einsum("qhd,kd->hqk", query, key, preferred_element_type=f32) * scale_factor
        weights = jnp.where(allowed[None], jnp.exp(logits), 0.0)
        probs = weights / jnp.sum(weights, axis=2, keepdims=True)
        probs_bf = probs.astype(bf16)
        heads = jnp.einsum("hqk,kd->qhd", probs_bf, value, preferred_element_type=f32)
        heads = heads.reshape(seq_rows, query_width).astype(bf16)

        def both_cores(partial):
            return partial + swap_col(partial.astype(bf16)).astype(f32)

        attn_proj = both_cores(dot(heads, w_out_t, ((1,), (1,))))
        scale_y = rms_scale(attn_proj)
        resid_mid = x + attn_proj * scale_y * g_attn
        scale_mid = rms_scale(resid_mid)
        ffn_in = (resid_mid * scale_mid * g_pre).astype(bf16)
        gate_up = dot(ffn_in, w_mix)
        gate_value = gate_up[:, :hidden_width]
        up_value = gate_up[:, hidden_width:]
        gelu_value, gelu_pull = jax.vjp(gelu_tanh, gate_value)
        hidden = (gelu_value * up_value).astype(bf16)
        ffn_out = both_cores(dot(hidden, w_down_t, ((1,), (1,))))
        scale_f = rms_scale(ffn_out)
        block_out = resid_mid + ffn_out * scale_f * g_post

        def place_out(full):
            return jnp.where(diag, full[:, :half_width], diag_to_off_row(full[:, half_width:]))

        block_output = place_out(block_out)

        def grad_sum(left, right):
            contract = ((0,), (0,))
            away = dot(left[:, half_width:], right, contract).astype(bf16)
            cur = dot(left[:, :half_width], right, contract) + swap_row(away).astype(f32)
            for bit in bits:
                rows = cur.shape[0]
                halves = cur.reshape(2, rows // 2, cur.shape[1])
                b = bit_of(bit)
                keep = lax.dynamic_index_in_dim(halves, b, 0, keepdims=False)
                send = lax.dynamic_index_in_dim(halves, 1 - b, 0, keepdims=False)
                cur = keep + swap_dp(send.astype(bf16), bit).astype(f32)
            cur = cur.astype(bf16)
            for bit in reversed(bits):
                b = bit_of(bit)
                theirs = swap_dp(cur, bit)
                cur = jnp.concatenate(
                    [jnp.where(b == 0, cur, theirs), jnp.where(b == 0, theirs, cur)], axis=0
                )
            return cur.astype(f32)

        grad_ffn, post_part = norm_back(cotangent, ffn_out, scale_f, g_post)
        grad_ffn = grad_ffn.astype(bf16)
        down_sum = grad_sum(grad_ffn, hidden).T
        grad_hidden = dot(grad_ffn, w_down_t)
        grad_gate = gelu_pull(grad_hidden * up_value)[0]
        grad_up = grad_hidden * gelu_value
        grad_mix = jnp.concatenate([grad_gate, grad_up], axis=1).astype(bf16)
        mix_sum = grad_sum(ffn_in, grad_mix)
        grad_pre = both_cores(dot(grad_mix, w_mix, ((1,), (1,))))
        grad_mid_norm, pre_part = norm_back(grad_pre, resid_mid, scale_mid, g_pre)
        grad_mid = cotangent + grad_mid_norm
        grad_attn, attn_part = norm_back(grad_mid, attn_proj, scale_y, g_attn)
        grad_attn = grad_attn.astype(bf16)
        out_sum = grad_sum(grad_attn, heads).T
        grad_heads = dot(grad_attn, w_out_t).astype(bf16)
        grad_heads = grad_heads.reshape(seq_rows, head_count, head_size)

        value_part = jnp.einsum("hqk,qhd->kd", probs_bf, grad_heads, preferred_element_type=f32)
        grad_probs = jnp.einsum("qhd,kd->hqk", grad_heads, value, preferred_element_type=f32)
        delta = jnp.sum(probs * grad_probs, axis=2, keepdims=True)
        grad_scores = (probs * (grad_probs - delta)).astype(bf16)
        grad_query_rot = (
            jnp.einsum("hqk,kd->qhd", grad_scores, key, preferred_element_type=f32) * scale_factor
        )
        key_part = (
            jnp.einsum("hqk,qhd->kd", grad_scores, query, preferred_element_type=f32)
            * scale_factor
        )
        kv_received = swap_col(jnp.where(first_col, value_part, key_part))
        kv_total = jnp.where(first_col, key_part, value_part) + kv_received
        grad_raw_query, query_gain_part = jax.vjp(query_map, raw_query, gain_query)[1](
            grad_query_rot
        )
        grad_raw_key, key_gain_part = jax.vjp(key_map, raw_key, gain_key)[1](kv_total)
        kv_grad = jnp.where(first_col, grad_raw_key, kv_total)
        grad_joint = jnp.concatenate(
            [grad_raw_query.reshape(seq_rows, query_width), kv_grad], axis=1
        ).astype(bf16)
        joint_sum = grad_sum(normed, grad_joint)
        grad_in = both_cores(dot(grad_joint, w_joint, ((1,), (1,))))
        grad_x_norm, input_part = norm_back(grad_in, x, scale_in, g_in)
        input_grad = place_out(grad_mid + grad_x_norm)

        query_sum = joint_sum[:, :query_width]
        kv_sum = joint_sum[:, query_width:]
        kv_sum_theirs = swap_col(kv_sum.astype(bf16)).astype(f32)
        key_sum = jnp.where(first_col, kv_sum, kv_sum_theirs)
        value_sum = jnp.where(first_col, kv_sum_theirs, kv_sum)

        width_parts = jnp.stack([input_part, attn_part, pre_part, post_part])
        width_parts = jnp.where(diag, width_parts, 0.0)
        key_gain_part = jnp.where(first_col, key_gain_part, 0.0)
        away = jnp.concatenate(
            [width_parts[:, half_width:].reshape(-1), query_gain_part, key_gain_part]
        )
        own = jnp.concatenate(
            [width_parts[:, :half_width].reshape(-1), query_gain_part, key_gain_part]
        )
        small = own + swap_row(away)
        small = small + swap_col(small)
        for bit in bits:
            small = small + swap_dp(small, bit)
        width_sums = small[: 4 * half_width].reshape(4, half_width)
        query_gain_sum = small[4 * half_width : 4 * half_width + head_size]
        key_gain_sum = small[4 * half_width + head_size :]
        return (
            block_output, input_grad, query_sum, key_sum, value_sum, out_sum,
            mix_sum[:, :hidden_width], mix_sum[:, hidden_width:], down_sum,
            width_sums[0], width_sums[1], width_sums[2], width_sums[3],
            query_gain_sum, key_gain_sum,
        )

    return step


def solution(mesh):
    rows_by_width = P(("dp", "col"), "row")
    in_specs = (
        rows_by_width, P(("dp", "row"), None), P("row", "col"), P("row", None), P("row", None),
        P("col", "row"), P("row", "col"), P("row", "col"), P("col", "row"),
        P("row"), P("row"), P("row"), P("row"), P(), P(), rows_by_width,
    )
    out_specs = (
        rows_by_width, rows_by_width, P("row", "col"), P("row", None), P("row", None),
        P("col", "row"), P("row", "col"), P("row", "col"), P("col", "row"),
        P("row"), P("row"), P("row"), P("row"), P(), P(),
    )
    return jax.shard_map(
        make_step(mesh), mesh=mesh, in_specs=in_specs, out_specs=out_specs, check_vma=False
    )
```

```python
import jax
import jax.numpy as jnp
from jax import lax
from jax.experimental import pallas as pl
from jax.experimental.pallas import tpu as pltpu
from jax.sharding import PartitionSpec as P

eps_norm = 1e-06
rope_base = 1000000.0
bf16 = jnp.bfloat16
f32 = jnp.float32
gelu_c = (2.0 / 3.141592653589793) ** 0.5
gelu_a = 0.044715


PLAN = {
    "down": ("y", 1, 2, 4),
    "gate": (1, 2, "y", 4),
    "up": (2, "y", 1, 4),
    "attn": (1, "y", 2, 4),
}
GATHER = {"down": (4, 2, 1), "gate": (4, 2, 1), "up": (4, 1, 2), "attn": (4, 1, 2)}


def dot(left, right, contract=((1,), (0,))):
    return lax.dot_general(left, right, (contract, ((), ())), preferred_element_type=f32)


def rms_scale(values):
    return lax.rsqrt(jnp.mean(values * values, axis=-1, keepdims=True) + eps_norm)


def norm_back(upstream, values, inv_rms, gain_vector):
    weighted = upstream * gain_vector
    width_sum = jnp.sum(weighted * values, axis=1, keepdims=True)
    through = inv_rms * weighted - values * (inv_rms**3 * width_sum / values.shape[1])
    return through, jnp.sum(upstream * values * inv_rms, axis=0, keepdims=True)


def rotate(values, cosine_table, sine_table):
    half = values.shape[1] // 2
    a, b = values[:, :half], values[:, half:]
    return jnp.concatenate(
        [a * cosine_table - b * sine_table, b * cosine_table + a * sine_table], axis=1
    )


def rotate_back(values, cosine_table, sine_table):
    return rotate(values, cosine_table, -sine_table)


def gelu_parts(v):
    t = jnp.tanh(gelu_c * (v + gelu_a * v * v * v))
    return t, 0.5 * v * (1.0 + t)


def call(body, outs, *args, scalars=None, scratch=()):
    in_specs = [pl.BlockSpec(memory_space=pltpu.VMEM) for _ in args]
    if scalars is not None:
        in_specs = [pl.BlockSpec(memory_space=pltpu.SMEM)] + in_specs
        args = (scalars,) + args
    return pl.pallas_call(
        body,
        in_specs=in_specs,
        out_specs=[pl.BlockSpec(memory_space=pltpu.VMEM) for _ in outs],
        out_shape=[jax.ShapeDtypeStruct(s, d) for s, d in outs],
        scratch_shapes=list(scratch),
    )(*args)


def proj_body(x, g, w, normed, raw_q, kv):
    v = x[...]
    n = (v * rms_scale(v) * g[0:1, :]).astype(bf16)
    normed[...] = n
    p = dot(n, w[...])
    qw = raw_q.shape[1]
    raw_q[...] = p[:, :qw]
    kv[...] = p[:, qw:]


def attn_body(sc, raw_q, kv_mine, kv_theirs, mask, cos, sin, gq, gk, w, q, k, v, probs, heads,
              part, send):
    first = sc[0] == 1
    c, s = cos[...], sin[...]
    hd = k.shape[1]
    raw_k = jnp.where(first, kv_mine[...], kv_theirs[...])
    raw_v = jnp.where(first, kv_theirs[...], kv_mine[...])
    key = rotate(raw_k * rms_scale(raw_k) * gk[...], c, s).astype(bf16)
    value = raw_v.astype(bf16)
    k[...] = key
    v[...] = value
    allowed = mask[...] > 0.0
    for h in range(q.shape[1] // hd):
        raw = raw_q[:, h * hd : (h + 1) * hd]
        query = rotate(raw * rms_scale(raw) * gq[...], c, s).astype(bf16)
        q[:, h * hd : (h + 1) * hd] = query
        logits = dot(query, key, ((1,), (1,))) * (hd**-0.5)
        weights = jnp.where(allowed, jnp.exp(logits), 0.0)
        p = weights / jnp.sum(weights, axis=1, keepdims=True)
        probs[h] = p
        heads[:, h * hd : (h + 1) * hd] = dot(p.astype(bf16), value).astype(bf16)
    out = dot(heads[...], w[...], ((1,), (1,)))
    part[...] = out
    send[...] = out.astype(bf16)


def mix_body(x, own, recv, g, w_gate, w_up, proj, mid, ffn_in, gate, up, hidden):
    y = own[...] + recv[...].astype(f32)
    proj[...] = y
    m = x[...] + y * rms_scale(y) * g[1:2, :]
    mid[...] = m
    n = (m * rms_scale(m) * g[2:3, :]).astype(bf16)
    ffn_in[...] = n
    ga = dot(n, w_gate[...])
    gate[...] = ga
    u = dot(n, w_up[...])
    up[...] = u
    hidden[...] = (gelu_parts(ga)[1] * u).astype(bf16)


def down_body(hidden, w, part, send):
    out = dot(hidden[...], w[...], ((1,), (1,)))
    part[...] = out
    send[...] = out.astype(bf16)


def split_grad(sc, left_t, right, send, keep, acc, plan, col=None):
    g = dot(left_t, right)
    n = g.shape[1]
    cols = slice(0, n) if col is None else slice(col, col + n)
    half = g.shape[0] // 2
    if plan == "y":
        send[:, cols] = g[half:].astype(bf16)
        keep[:, cols] = g[:half]
        return
    pieces = 2 if plan == 1 else 4
    rows = half // pieces
    acc[:, :, cols] = g.reshape(2 * pieces, rows, n)
    b = sc[plan]
    for i in range(pieces):
        mine, theirs = 2 * i + b, 2 * i + 1 - b
        send[i, :, cols] = acc[theirs, :, cols].astype(bf16)
        keep[i, :, cols] = acc[mine, :, cols]


def grad_shapes(plan, width, n):
    half = width // 2
    if plan == "y":
        return ((half, n), (half, n)), None
    pieces = 2 if plan == 1 else 4
    rows = half // pieces
    return ((pieces, rows, n), (pieces, rows, n)), (2 * pieces, rows, n)


def down_grad_body(sc, mid, own, recv, cot, g, hidden, out, grad_ffn, gain_part, send, keep):
    f = own[...] + recv[...].astype(f32)
    s = rms_scale(f)
    out[...] = mid[...] + f * s * g[3:4, :]
    through, part = norm_back(cot[...], f, s, g[3:4, :])
    gain_part[...] = part
    gf = through.astype(bf16)
    grad_ffn[...] = gf
    split_grad(sc, gf.T, hidden[...], send, keep, None, PLAN["down"][0])


def gate_grad_body(sc, grad_ffn, w, gate, up, ffn_in, grad_gate, grad_up, send, keep, acc):
    gh = dot(grad_ffn[...], w[...])
    v = gate[...]
    t, gelu = gelu_parts(v)
    slope = 0.5 * (1.0 + t) + 0.5 * v * (1.0 - t * t) * (gelu_c * (1.0 + 3.0 * gelu_a * v * v))
    gg = (gh * up[...] * slope).astype(bf16)
    grad_gate[...] = gg
    grad_up[...] = (gh * gelu).astype(bf16)
    split_grad(sc, ffn_in[...].T, gg, send, keep, acc, PLAN["gate"][0])


def up_grad_body(sc, ffn_in, grad_up, send, keep, acc):
    split_grad(sc, ffn_in[...].T, grad_up[...], send, keep, acc, PLAN["up"][0])


def pre_body(grad_gate, grad_up, w_gate, w_up, part, send):
    out = dot(grad_gate[...], w_gate[...], ((1,), (1,))) + dot(
        grad_up[...], w_up[...], ((1,), (1,))
    )
    part[...] = out
    send[...] = out.astype(bf16)


def attn_grad_body(sc, own, recv, mid, proj, cot, g, w, q, k, v, probs, raw_q, cos, sin, gq,
                   grad_mid, grad_attn, pre_part, attn_part, kv_own, kv_send, grad_q, q_part):
    up = own[...] + recv[...].astype(f32)
    m = mid[...]
    through, part = norm_back(up, m, rms_scale(m), g[2:3, :])
    pre_part[...] = part
    gm = cot[...] + through
    grad_mid[...] = gm
    y = proj[...]
    through, part = norm_back(gm, y, rms_scale(y), g[1:2, :])
    attn_part[...] = part
    ga = through.astype(bf16)
    grad_attn[...] = ga
    grad_heads = dot(ga, w[...]).astype(bf16)
    hd = k.shape[1]
    c, s = cos[...], sin[...]
    key, value = k[...], v[...]
    value_part, key_part, gain_part = 0.0, 0.0, 0.0
    scale = hd**-0.5
    for h in range(q.shape[1] // hd):
        cols = slice(h * hd, (h + 1) * hd)
        gh = grad_heads[:, cols]
        p = probs[h]
        value_part = value_part + dot(p.astype(bf16).T, gh)
        gp = dot(gh, value, ((1,), (1,)))
        delta = jnp.sum(p * gp, axis=1, keepdims=True)
        gs = (p * (gp - delta)).astype(bf16)
        gq_rot = dot(gs, key) * scale
        key_part = key_part + dot(gs.T, q[:, cols]) * scale
        raw = raw_q[:, cols]
        through, part = norm_back(rotate_back(gq_rot, c, s), raw, rms_scale(raw), gq[...])
        grad_q[:, cols] = through.astype(bf16)
        gain_part = gain_part + part
    q_part[...] = gain_part
    first = sc[0] == 1
    kv_own[...] = jnp.where(first, key_part, value_part)
    kv_send[...] = jnp.where(first, value_part, key_part)


def joint_body(sc, kv_own, kv_recv, kv_raw, cos, sin, gk, grad_q, normed, grad_attn, heads, w,
               k_part, send, keep, part, part_send, acc):
    total = kv_own[...] + kv_recv[...]
    raw = kv_raw[...]
    through, gain_part = norm_back(
        rotate_back(total, cos[...], sin[...]), raw, rms_scale(raw), gk[...]
    )
    first = sc[0] == 1
    k_part[...] = jnp.where(first, gain_part, 0.0)
    kvg = jnp.where(first, through, total).astype(bf16)
    gq = grad_q[...]
    qw = gq.shape[1]
    nt = normed[...].T
    kw = kvg.shape[1]
    plan = PLAN["attn"][0]
    split_grad(sc, nt, gq, send, keep, acc, plan, 0)
    split_grad(sc, nt, kvg, send, keep, acc, plan, qw)
    split_grad(sc, grad_attn[...].T, heads[...], send, keep, acc, plan, qw + kw)
    out = dot(gq, w[:, :qw], ((1,), (1,))) + dot(kvg, w[:, qw:], ((1,), (1,)))
    part[...] = out
    part_send[...] = out.astype(bf16)


def input_body(own, recv, x, grad_mid, g, out, gain_part):
    up = own[...] + recv[...].astype(f32)
    v = x[...]
    through, part = norm_back(up, v, rms_scale(v), g[0:1, :])
    out[...] = grad_mid[...] + through
    gain_part[...] = part


def make_step(mesh):
    n_dp, n_row, n_col = mesh.shape["dp"], mesh.shape["row"], mesh.shape["col"]
    assert n_row == 2 and n_col == 2 and n_dp >= 8
    bits = []
    while (1 << len(bits)) < n_dp:
        bits.append(1 << len(bits))
    assert (1 << len(bits)) == n_dp
    extra = tuple(b for b in bits if b > 4)

    def swap_row(v):
        return lax.ppermute(v, "row", [(0, 1), (1, 0)])

    def swap_col(v):
        return lax.ppermute(v, "col", [(0, 1), (1, 0)])

    def swap_dp(v, bit):
        return lax.ppermute(v, "dp", [(i, i ^ bit) for i in range(n_dp)])

    def step(
        block_input, segment_ids, w_query, w_key, w_value, w_out, w_gate, w_up, w_down,
        gain_input, gain_attn, gain_ffn_pre, gain_ffn_post, gain_query, gain_key, out_cotangent,
    ):
        rows, half_width = block_input.shape
        width = 2 * half_width
        hd = w_key.shape[1]
        qw = w_query.shape[1]
        n_head = qw // hd
        ff = w_gate.shape[1]
        row = lax.axis_index("row")
        col = lax.axis_index("col")
        dp = lax.axis_index("dp")
        diag = row == col
        first_col = col == 0

        def bit_of(bit):
            return (dp // bit) % 2

        code = (1 - col) + 2 * bit_of(1) + 4 * bit_of(2)
        sc = (code >> jnp.arange(4, dtype=jnp.int32)) & 1

        def off_to_diag(v):
            return lax.ppermute(v, ("row", "col"), [(1, 3), (2, 0)])

        def diag_to_off_col(v):
            return lax.ppermute(v, ("row", "col"), [(0, 1), (3, 2)])

        def diag_to_off_row(v):
            return lax.ppermute(v, ("row", "col"), [(0, 2), (3, 1)])

        def chip_sequence(local):
            other_diag = off_to_diag(local)
            own = jnp.where(diag, local, diag_to_off_col(local))
            other = jnp.where(diag, other_diag, diag_to_off_col(other_diag))
            return jnp.concatenate([own, other], axis=1)

        def with_other_rows(own, first_bit, second_bit):
            n = own.shape[1]
            q = own.shape[0] // 4
            pieces = own.reshape(2, 2, q, n)
            b1, b2 = bit_of(1), bit_of(2)
            part = lax.dynamic_slice(pieces, (b2, b1, 0, 0), (1, 1, q, n))
            cur = swap_row(part)
            for bit in (first_bit, second_bit):
                axis = 1 if bit == 1 else 0
                b = b1 if bit == 1 else b2
                theirs = swap_dp(cur, bit)
                cur = jnp.concatenate(
                    [jnp.where(b == 0, cur, theirs), jnp.where(b == 0, theirs, cur)], axis=axis
                )
            return jnp.concatenate([own, cur.reshape(4 * q, n)], axis=0)

        gains_own = jnp.concatenate(
            [v[None] for v in (gain_input, gain_attn, gain_ffn_pre, gain_ffn_post)], axis=0
        )
        gains = jnp.concatenate([gains_own, swap_row(gains_own)], axis=1)
        x = chip_sequence(block_input)
        joint_own = jnp.concatenate([w_query, jnp.where(first_col, w_key, w_value)], axis=1)
        w_joint = jnp.concatenate([joint_own, swap_row(joint_own)], axis=0)
        wg = with_other_rows(w_gate, 1, 2)
        wu = with_other_rows(w_up, 2, 1)
        out_own = w_out.T
        wo = jnp.concatenate([out_own, swap_row(out_own)], axis=0)
        wd = with_other_rows(w_down.T, 1, 2)
        cotangent = chip_sequence(out_cotangent)

        segments = segment_ids[0]
        places = jnp.arange(rows, dtype=jnp.int32)
        allowed = (segments[:, None] == segments[None, :]) & (places[:, None] >= places[None, :])
        mask = allowed.astype(f32)
        offsets = jnp.sum(mask, axis=1) - 1.0
        frequency = rope_base ** (-(jnp.arange(hd // 2, dtype=f32) * 2.0 / hd))
        angles = offsets[:, None] * frequency
        cos, sin = jnp.cos(angles), jnp.sin(angles)
        gq, gk = gain_query[None], gain_key[None]

        t = rows
        normed, raw_q, kv_mine = call(
            proj_body, [((t, width), bf16), ((t, qw), f32), ((t, hd), f32)],
            x, gains, w_joint,
        )
        kv_theirs = swap_col(kv_mine)
        q, k, v, probs, heads, part, send = call(
            attn_body,
            [((t, qw), bf16), ((t, hd), bf16), ((t, hd), bf16), ((n_head, t, t), f32),
             ((t, qw), bf16), ((t, width), f32), ((t, width), bf16)],
            raw_q, kv_mine, kv_theirs, mask, cos, sin, gq, gk, wo, scalars=sc,
        )
        proj, mid, ffn_in, gate, up, hidden = call(
            mix_body,
            [((t, width), f32), ((t, width), f32), ((t, width), bf16), ((t, ff), f32),
             ((t, ff), f32), ((t, ff), bf16)],
            x, part, swap_col(send), gains, wg, wu,
        )
        part, send = call(down_body, [((t, width), f32), ((t, width), bf16)], hidden, wd)

        def first_shapes(name, n):
            (a, b), s = grad_shapes(PLAN[name][0], width, n)
            return [(a, bf16), (b, f32)], [] if s is None else [pltpu.VMEM(s, f32)]

        axis_of = {"y": 0}
        for i, bit in enumerate(bits):
            axis_of[bit] = i + 1
        block = half_width // n_dp

        def swap(v, d):
            return swap_row(v) if d == "y" else swap_dp(v, d)

        def take(cur, d, which):
            if d == "y":
                return cur[which : which + 1]
            b = bit_of(d)
            return lax.dynamic_slice_in_dim(cur, b if which == 0 else 1 - b, 1, axis_of[d])

        def grad_sum(name, send, keep):
            n = keep.shape[-1]
            order = PLAN[name] + extra
            sizes = [2] * (len(bits) + 1)
            sizes[axis_of[order[0]]] = 1
            shape = tuple(sizes) + (block, n)
            cur = keep.reshape(shape)
            cur = cur + swap(send.reshape(shape), order[0]).astype(f32)
            for d in order[1:]:
                sent = take(cur, d, 1).astype(bf16)
                cur = take(cur, d, 0) + swap(sent, d).astype(f32)
            cur = cur.astype(bf16)
            for d in tuple(reversed(extra)) + GATHER[name]:
                theirs = swap(cur, d)
                b = bit_of(d)
                cur = jnp.concatenate(
                    [jnp.where(b == 0, cur, theirs), jnp.where(b == 0, theirs, cur)],
                    axis=axis_of[d],
                )
            return cur.reshape(half_width, n).astype(f32)

        def place_out(full):
            return jnp.where(diag, full[:, :half_width], diag_to_off_row(full[:, half_width:]))

        outs, scr = first_shapes("down", ff)
        block_out, grad_ffn, post_part, s_down, k_down = call(
            down_grad_body,
            [((t, width), f32), ((t, width), bf16), ((1, width), f32)] + outs,
            mid, part, swap_col(send), cotangent, gains, hidden, scalars=sc, scratch=scr,
        )
        down_sum = grad_sum("down", s_down, k_down)
        outs, scr = first_shapes("gate", ff)
        grad_gate, grad_up, s_gate, k_gate = call(
            gate_grad_body, [((t, ff), bf16), ((t, ff), bf16)] + outs,
            grad_ffn, wd, gate, up, ffn_in, scalars=sc, scratch=scr,
        )
        gate_sum = grad_sum("gate", s_gate, k_gate)
        outs, scr = first_shapes("up", ff)
        s_up, k_up = call(up_grad_body, outs, ffn_in, grad_up, scalars=sc, scratch=scr)
        up_sum = grad_sum("up", s_up, k_up)
        part, send = call(
            pre_body, [((t, width), f32), ((t, width), bf16)],
            grad_gate, grad_up, wg, wu,
        )
        block_output = place_out(block_out)
        grad_mid, grad_attn, pre_part, attn_part, kv_own, kv_send, grad_q, q_part = call(
            attn_grad_body,
            [((t, width), f32), ((t, width), bf16), ((1, width), f32), ((1, width), f32),
             ((t, hd), f32), ((t, hd), f32), ((t, qw), bf16), ((1, hd), f32)],
            part, swap_col(send), mid, proj, cotangent, gains, wo, q, k, v, probs,
            raw_q, cos, sin, gq, scalars=sc,
        )
        outs, scr = first_shapes("attn", qw + hd + qw)
        k_part, s_attn, k_attn, part, send = call(
            joint_body,
            [((1, hd), f32)] + outs + [((t, width), f32), ((t, width), bf16)],
            kv_own, swap_col(kv_send), kv_mine, cos, sin, gk, grad_q, normed,
            grad_attn, heads, w_joint, scalars=sc, scratch=scr,
        )
        attn_sum = grad_sum("attn", s_attn, k_attn)
        in_grad, in_part = call(
            input_body, [((t, width), f32), ((1, width), f32)],
            part, swap_col(send), x, grad_mid, gains,
        )
        input_grad = place_out(in_grad)

        query_sum = attn_sum[:, :qw]
        kv_sum = attn_sum[:, qw : qw + hd]
        out_sum = attn_sum[:, qw + hd :]
        kv_sum_theirs = swap_col(kv_sum.astype(bf16)).astype(f32)
        key_sum = jnp.where(first_col, kv_sum, kv_sum_theirs)
        value_sum = jnp.where(first_col, kv_sum_theirs, kv_sum)

        width_parts = jnp.concatenate([in_part, attn_part, pre_part, post_part], axis=0)
        width_parts = jnp.where(diag, width_parts, 0.0)
        ends = [q_part[0], k_part[0]]
        own = jnp.concatenate([width_parts[:, :half_width].reshape(-1)] + ends)
        away = jnp.concatenate([width_parts[:, half_width:].reshape(-1)] + ends)
        small = own + swap_row(away)
        small = small + swap_col(small)
        for bit in bits:
            small = small + swap_dp(small, bit)
        width_sums = small[: 4 * half_width].reshape(4, half_width)
        return (
            block_output, input_grad, query_sum, key_sum, value_sum, out_sum.T,
            gate_sum, up_sum, down_sum.T,
            width_sums[0], width_sums[1], width_sums[2], width_sums[3],
            small[4 * half_width : 4 * half_width + hd], small[4 * half_width + hd :],
        )

    return step


def solution(mesh):
    rows_by_width = P(("dp", "col"), "row")
    in_specs = (
        rows_by_width, P(("dp", "row"), None), P("row", "col"), P("row", None), P("row", None),
        P("col", "row"), P("row", "col"), P("row", "col"), P("col", "row"),
        P("row"), P("row"), P("row"), P("row"), P(), P(), rows_by_width,
    )
    out_specs = (
        rows_by_width, rows_by_width, P("row", "col"), P("row", None), P("row", None),
        P("col", "row"), P("row", "col"), P("row", "col"), P("col", "row"),
        P("row"), P("row"), P("row"), P("row"), P(), P(),
    )
    return jax.shard_map(
        make_step(mesh), mesh=mesh, in_specs=in_specs, out_specs=out_specs, check_vma=False
    )
```

```python
import jax
import jax.numpy as jnp
from jax import lax
from jax.experimental import pallas as pl
from jax.experimental.pallas import tpu as pltpu
from jax.sharding import PartitionSpec as P

eps_norm = 1e-06
rope_base = 1000000.0
bf16 = jnp.bfloat16
f32 = jnp.float32
gelu_c = (2.0 / 3.141592653589793) ** 0.5
gelu_a = 0.044715


PLAN = {
    "down": ("y", 1, 2, 4),
    "gate": (2, "y", 1, 4),
    "up": (1, "y", 2, 4),
    "attn": (2, "y", 1, 4),
}
GATHER = {"down": (4, 2, 1), "gate": (4, 2, 1), "up": (4, 2, 1), "attn": (4, 1, 2)}
TOP_BITS = (1, 2, 4)


def dot(left, right, contract=((1,), (0,))):
    return lax.dot_general(left, right, (contract, ((), ())), preferred_element_type=f32)


def rms_scale(values):
    return lax.rsqrt(jnp.mean(values * values, axis=-1, keepdims=True) + eps_norm)


def norm_back(upstream, values, inv_rms, gain_vector):
    weighted = upstream * gain_vector
    width_sum = jnp.sum(weighted * values, axis=1, keepdims=True)
    through = inv_rms * weighted - values * (inv_rms**3 * width_sum / values.shape[1])
    return through, jnp.sum(upstream * values * inv_rms, axis=0, keepdims=True)


def rotate(values, cosine_table, sine_table):
    half = values.shape[1] // 2
    a, b = values[:, :half], values[:, half:]
    return jnp.concatenate(
        [a * cosine_table - b * sine_table, b * cosine_table + a * sine_table], axis=1
    )


def rotate_back(values, cosine_table, sine_table):
    return rotate(values, cosine_table, -sine_table)


def gelu_parts(v):
    t = jnp.tanh(gelu_c * (v + gelu_a * v * v * v))
    return t, 0.5 * v * (1.0 + t)


def call(body, outs, *args, scalars=None, scratch=(), out_hbm=False, limit=24):
    in_specs = [pl.BlockSpec(memory_space=pltpu.VMEM) for _ in args]
    args = tuple(pltpu.with_memory_space_constraint(v, pltpu.VMEM) for v in args)
    if scalars is not None:
        in_specs = [pl.BlockSpec(memory_space=pltpu.SMEM)] + in_specs
        args = (scalars,) + args
    place = jax.ShapeDtypeStruct if out_hbm else pltpu.VMEM
    return pl.pallas_call(
        body,
        in_specs=in_specs,
        out_specs=[pl.BlockSpec(memory_space=pltpu.VMEM) for _ in outs],
        out_shape=[place(s, d) for s, d in outs],
        scratch_shapes=list(scratch),
        compiler_params=pltpu.CompilerParams(vmem_limit_bytes=limit << 20),
    )(*args)


def join_rows(scr, own, other):
    half = own.shape[0]
    scr[:half, :] = own[...]
    scr[half:, :] = other[...]


def place_rows(scr, sc, pieces, first_bit):
    own, near, first, second = pieces
    half, q = own.shape[0], near.shape[0]
    scr[:half, :] = own[...]
    b1, b2 = sc[1], sc[2]

    def at(r1, r2):
        p1 = 1 - b1 if r1 else b1
        p2 = 1 - b2 if r2 else b2
        return pl.ds(pl.multiple_of(half + q * (2 * p2 + p1), 16), q)

    scr[at(0, 0), :] = near[...]
    scr[at(1, 0) if first_bit == 1 else at(0, 1), :] = first[...]
    scr[at(0, 1) if first_bit == 1 else at(1, 0), :] = second[:q, :]
    scr[at(1, 1), :] = second[q:, :]


def sequence_t(sc, local, own_recv, diag_recv, other_recv):
    diag = sc[3] == 1
    own = jnp.where(diag, local[...], own_recv[...].astype(f32))
    other = jnp.where(diag, diag_recv[...].astype(f32), other_recv[...].astype(f32))
    return jnp.concatenate([own, other], axis=0).T


def proj_body(sc, x_local, x_own, x_diag, x_other, g, w_own, w_other, x, normed, raw_q, kv, w):
    join_rows(w, w_own, w_other)
    v = sequence_t(sc, x_local, x_own, x_diag, x_other)
    x[...] = v
    n = (v * rms_scale(v) * g[0:1, :]).astype(bf16)
    normed[...] = n
    p = dot(n, w[...])
    qw = raw_q.shape[1]
    raw_q[...] = p[:, :qw]
    kv[...] = p[:, qw:]


def cot_body(sc, c_local, c_own, c_diag, c_other, cot):
    cot[...] = sequence_t(sc, c_local, c_own, c_diag, c_other)


def attn_body(sc, raw_q, kv_mine, kv_theirs, mask, cos, sin, gq, gk, w_own, w_other, q, k, v,
              probs, heads, part, send, w):
    join_rows(w, w_own, w_other)
    first = sc[0] == 1
    c, s = cos[...], sin[...]
    hd = k.shape[1]
    raw_k = jnp.where(first, kv_mine[...], kv_theirs[...])
    raw_v = jnp.where(first, kv_theirs[...], kv_mine[...])
    key = rotate(raw_k * rms_scale(raw_k) * gk[...], c, s).astype(bf16)
    value = raw_v.astype(bf16)
    k[...] = key
    v[...] = value
    allowed = mask[...] > 0.0
    for h in range(q.shape[1] // hd):
        raw = raw_q[:, h * hd : (h + 1) * hd]
        query = rotate(raw * rms_scale(raw) * gq[...], c, s).astype(bf16)
        q[:, h * hd : (h + 1) * hd] = query
        logits = dot(query, key, ((1,), (1,))) * (hd**-0.5)
        weights = jnp.where(allowed, jnp.exp(logits), 0.0)
        p = weights / jnp.sum(weights, axis=1, keepdims=True)
        probs[h] = p
        heads[:, h * hd : (h + 1) * hd] = dot(p.astype(bf16), value).astype(bf16)
    out = dot(heads[...], w[...], ((1,), (1,)))
    part[...] = out
    send[...] = out.astype(bf16)


def mix_body(sc, x, own, recv, g, *refs):
    wg_p, wu_p = refs[0:4], refs[4:8]
    proj, mid, ffn_in, gate, up, hidden, wg, wu = refs[8:]
    place_rows(wg, sc, wg_p, 1)
    place_rows(wu, sc, wu_p, 2)
    y = own[...] + recv[...].astype(f32)
    proj[...] = y
    m = x[...] + y * rms_scale(y) * g[1:2, :]
    mid[...] = m
    n = (m * rms_scale(m) * g[2:3, :]).astype(bf16)
    ffn_in[...] = n
    ga = dot(n, wg[...])
    gate[...] = ga
    u = dot(n, wu[...])
    up[...] = u
    hidden[...] = (gelu_parts(ga)[1] * u).astype(bf16)


def down_body(sc, hidden, *refs):
    wd_p = refs[0:4]
    part, send, wd = refs[4:]
    place_rows(wd, sc, wd_p, 1)
    out = dot(hidden[...], wd[...], ((1,), (1,)))
    part[...] = out
    send[...] = out.astype(bf16)


def split_axis(sc, src, blocks, rows, left, d, emit):
    if d == "y":
        emit(0, 0, src(0, 0, rows), src(1, 0, rows))
        return
    groups = 1 << left.index(d)
    size = rows // groups
    half = size // 2
    b = sc[{1: 1, 2: 2, 4: 4}[d]]
    for block in range(blocks):
        for i in range(groups):
            mine = pl.multiple_of(i * size + b * half, 8)
            theirs = pl.multiple_of(i * size + (1 - b) * half, 8)
            emit(block, i * half, src(block, mine, half), src(block, theirs, half))


def split_grad(sc, left_t, right, send, keep, acc, d, col=0):
    g = dot(left_t, right)
    n = g.shape[1]
    cols = slice(col, col + n)
    half = g.shape[0] // 2
    if d == "y":
        send[0, :, cols] = g[half:].astype(bf16)
        keep[0, :, cols] = g[:half]
        return
    acc[0, :, cols] = g[:half]
    acc[1, :, cols] = g[half:]

    def emit(block, at, mine, theirs):
        rows = slice(at, at + mine.shape[0])
        send[block, rows, cols] = theirs.astype(bf16)
        keep[block, rows, cols] = mine

    split_axis(
        sc, lambda block, start, size: acc[block, pl.ds(start, size), cols], 2, half, TOP_BITS,
        d, emit,
    )


def stage_shapes(blocks, rows, n, d):
    if d == "y":
        return (1, rows, n)
    return (blocks, rows // 2, n)


def stage_body(d, left):
    def body(sc, keep_in, recv, send, keep, acc):
        blocks, rows, _ = keep_in.shape
        for block in range(blocks):
            acc[block] = keep_in[block] + recv[block].astype(f32)

        def emit(block, at, mine, theirs):
            span = slice(at, at + mine.shape[0])
            send[block, span, :] = theirs.astype(bf16)
            keep[block, span, :] = mine

        split_axis(
            sc, lambda block, start, size: acc[block, pl.ds(start, size), :], blocks, rows, left,
            d, emit,
        )

    return body


def last_sum_body(keep_in, recv, send):
    send[...] = (keep_in[...] + recv[...].astype(f32)).astype(bf16)


def assemble_body(order, widths):
    def body(sc, near, far, *outs):
        rows = near.shape[1]
        for part, ref in ((0, near), (1, far)):
            for j in range(4):
                rel = {order[0]: j & 1, order[1]: j >> 1, order[2]: part}
                pos = 0
                for bit in TOP_BITS:
                    b = sc[bit]
                    pos = 2 * pos + (1 - b if rel[bit] else b)
                at = pl.ds(pl.multiple_of(pos * rows, 8), rows)
                val = ref[j].astype(f32)
                col = 0
                for out, w in zip(outs, widths):
                    out[at, :] = val[:, col : col + w].astype(out.dtype)
                    col += w

    return body


def down_grad_body(sc, mid, own, recv, cot, g, hidden, out, out_send, grad_ffn, gain_part, send,
                   keep):
    f = own[...] + recv[...].astype(f32)
    s = rms_scale(f)
    full = (mid[...] + f * s * g[3:4, :]).T
    half = full.shape[0] // 2
    out[...] = full[:half]
    out_send[...] = full[half:].astype(bf16)
    through, part = norm_back(cot[...], f, s, g[3:4, :])
    gain_part[...] = part
    gf = through.astype(bf16)
    grad_ffn[...] = gf
    split_grad(sc, gf.T, hidden[...], send, keep, None, PLAN["down"][0])


def mix_grad_body(sc, grad_ffn, gate, up, ffn_in, *refs):
    wg_p, wu_p, wd_p = refs[0:4], refs[4:8], refs[8:12]
    s_gate, k_gate, s_up, k_up, part, send, wg, wu, wd, acc = refs[12:]
    place_rows(wd, sc, wd_p, 1)
    place_rows(wg, sc, wg_p, 1)
    place_rows(wu, sc, wu_p, 2)
    gh = dot(grad_ffn[...], wd[...])
    v = gate[...]
    t, gelu = gelu_parts(v)
    slope = 0.5 * (1.0 + t) + 0.5 * v * (1.0 - t * t) * (gelu_c * (1.0 + 3.0 * gelu_a * v * v))
    gg = (gh * up[...] * slope).astype(bf16)
    gu = (gh * gelu).astype(bf16)
    n_t = ffn_in[...].T
    split_grad(sc, n_t, gg, s_gate, k_gate, acc, PLAN["gate"][0])
    split_grad(sc, n_t, gu, s_up, k_up, acc, PLAN["up"][0])
    out = dot(gg, wg[...], ((1,), (1,))) + dot(gu, wu[...], ((1,), (1,)))
    part[...] = out
    send[...] = out.astype(bf16)


def attn_grad_body(sc, own, recv, mid, proj, cot, g, w_own, w_other, q, k, v, probs, raw_q, cos,
                   sin, gq, grad_mid, grad_attn, pre_part, attn_part, kv_own, kv_send, grad_q,
                   q_part, w):
    join_rows(w, w_own, w_other)
    up = own[...] + recv[...].astype(f32)
    m = mid[...]
    through, part = norm_back(up, m, rms_scale(m), g[2:3, :])
    pre_part[...] = part
    gm = cot[...] + through
    grad_mid[...] = gm
    y = proj[...]
    through, part = norm_back(gm, y, rms_scale(y), g[1:2, :])
    attn_part[...] = part
    ga = through.astype(bf16)
    grad_attn[...] = ga
    grad_heads = dot(ga, w[...]).astype(bf16)
    hd = k.shape[1]
    c, s = cos[...], sin[...]
    key, value = k[...], v[...]
    value_part, key_part, gain_part = 0.0, 0.0, 0.0
    scale = hd**-0.5
    for h in range(q.shape[1] // hd):
        cols = slice(h * hd, (h + 1) * hd)
        gh = grad_heads[:, cols]
        p = probs[h]
        value_part = value_part + dot(p.astype(bf16).T, gh)
        gp = dot(gh, value, ((1,), (1,)))
        delta = jnp.sum(p * gp, axis=1, keepdims=True)
        gs = (p * (gp - delta)).astype(bf16)
        gq_rot = dot(gs, key) * scale
        key_part = key_part + dot(gs.T, q[:, cols]) * scale
        raw = raw_q[:, cols]
        through, part = norm_back(rotate_back(gq_rot, c, s), raw, rms_scale(raw), gq[...])
        grad_q[:, cols] = through.astype(bf16)
        gain_part = gain_part + part
    q_part[...] = gain_part
    first = sc[0] == 1
    kv_own[...] = jnp.where(first, key_part, value_part)
    kv_send[...] = jnp.where(first, value_part, key_part)


def joint_body(sc, kv_own, kv_recv, kv_raw, cos, sin, gk, grad_q, normed, grad_attn, heads,
               w_own, w_other, k_part, send, keep, part, part_send, w, acc):
    join_rows(w, w_own, w_other)
    total = kv_own[...] + kv_recv[...]
    raw = kv_raw[...]
    through, gain_part = norm_back(
        rotate_back(total, cos[...], sin[...]), raw, rms_scale(raw), gk[...]
    )
    first = sc[0] == 1
    k_part[...] = jnp.where(first, gain_part, 0.0)
    kvg = jnp.where(first, through, total).astype(bf16)
    gq = grad_q[...]
    qw, kw = gq.shape[1], kvg.shape[1]
    n_t = normed[...].T
    d = PLAN["attn"][0]
    split_grad(sc, n_t, gq, send, keep, acc, d, 0)
    split_grad(sc, n_t, kvg, send, keep, acc, d, qw)
    split_grad(sc, grad_attn[...].T, heads[...], send, keep, acc, d, qw + kw)
    out = dot(gq, w[:, :qw], ((1,), (1,))) + dot(kvg, w[:, qw:], ((1,), (1,)))
    part[...] = out
    part_send[...] = out.astype(bf16)


def input_body(own, recv, x, grad_mid, g, out, out_send, gain_part):
    up = own[...] + recv[...].astype(f32)
    v = x[...]
    through, part = norm_back(up, v, rms_scale(v), g[0:1, :])
    full = (grad_mid[...] + through).T
    half = full.shape[0] // 2
    out[...] = full[:half]
    out_send[...] = full[half:].astype(bf16)
    gain_part[...] = part


def make_step(mesh):
    n_dp, n_row, n_col = mesh.shape["dp"], mesh.shape["row"], mesh.shape["col"]
    assert n_row == 2 and n_col == 2 and n_dp >= 8
    bits = []
    while (1 << len(bits)) < n_dp:
        bits.append(1 << len(bits))
    assert (1 << len(bits)) == n_dp
    extra = tuple(b for b in bits if b > 4)

    def swap_row(v):
        return lax.ppermute(v, "row", [(0, 1), (1, 0)])

    def swap_col(v):
        return lax.ppermute(v, "col", [(0, 1), (1, 0)])

    def swap_dp(v, bit):
        return lax.ppermute(v, "dp", [(i, i ^ bit) for i in range(n_dp)])

    def step(
        block_input, segment_ids, w_query, w_key, w_value, w_out, w_gate, w_up, w_down,
        gain_input, gain_attn, gain_ffn_pre, gain_ffn_post, gain_query, gain_key, out_cotangent,
    ):
        rows, half_width = block_input.shape
        width = 2 * half_width
        hd = w_key.shape[1]
        qw = w_query.shape[1]
        n_head = qw // hd
        ff = w_gate.shape[1]
        row = lax.axis_index("row")
        col = lax.axis_index("col")
        dp = lax.axis_index("dp")
        diag = row == col
        first_col = col == 0

        def bit_of(bit):
            return (dp // bit) % 2

        code = (1 - col) + 2 * bit_of(1) + 4 * bit_of(2) + 8 * (row == col) + 16 * bit_of(4)
        sc = (code >> jnp.arange(8, dtype=jnp.int32)) & 1

        def off_to_diag(v):
            return lax.ppermute(v, ("row", "col"), [(1, 3), (2, 0)])

        def diag_to_off_col(v):
            return lax.ppermute(v, ("row", "col"), [(0, 1), (3, 2)])

        def diag_to_off_row(v):
            return lax.ppermute(v, ("row", "col"), [(0, 2), (3, 1)])

        def chip_sequence(local, kind):
            local_t = local.T
            narrow = local_t.astype(kind)
            from_row = off_to_diag(narrow)
            return local_t, diag_to_off_col(narrow), from_row, diag_to_off_col(from_row)

        def with_other_rows(own, first_bit, second_bit):
            q = own.shape[0] // 4
            at = (2 * bit_of(2) + bit_of(1)) * q
            near = swap_row(lax.dynamic_slice_in_dim(own, at, q, 0))
            first = swap_dp(near, first_bit)
            second = swap_dp(jnp.concatenate([near, first], axis=0), second_bit)
            return own, near, first, second

        x_pieces = chip_sequence(block_input, f32)
        joint_own = jnp.concatenate([w_query, jnp.where(first_col, w_key, w_value)], axis=1)
        w_joint = (joint_own, swap_row(joint_own))
        which = lax.broadcasted_iota(jnp.int32, (4, half_width), 0)
        gains_own = jnp.where(
            which == 0, gain_input,
            jnp.where(which == 1, gain_attn, jnp.where(which == 2, gain_ffn_pre, gain_ffn_post)),
        )
        gains = jnp.concatenate([gains_own, swap_row(gains_own)], axis=1)
        wg = with_other_rows(w_gate, 1, 2)
        wu = with_other_rows(w_up, 2, 1)
        out_own = w_out.T
        wo = (out_own, swap_row(out_own))
        wd = with_other_rows(w_down.T, 1, 2)
        cot_pieces = chip_sequence(out_cotangent, bf16)

        segments = segment_ids[0]
        places = jnp.arange(rows, dtype=jnp.int32)
        allowed = (segments[:, None] == segments[None, :]) & (places[:, None] >= places[None, :])
        mask = allowed.astype(f32)
        offsets = jnp.sum(mask, axis=1) - 1.0
        frequency = rope_base ** (-(jnp.arange(hd // 2, dtype=f32) * 2.0 / hd))
        angles = offsets[:, None] * frequency
        cos, sin = jnp.cos(angles), jnp.sin(angles)
        gq, gk = gain_query[None], gain_key[None]

        t = rows
        joint_width = qw + hd
        wide_f, wide_b = ((t, width), f32), ((t, width), bf16)
        ffn_scratch = [pltpu.VMEM((width, ff), bf16) for _ in range(3)]
        x, normed, raw_q, kv_mine = call(
            proj_body, [wide_f, wide_b, ((t, qw), f32), ((t, hd), f32)],
            *x_pieces, gains, *w_joint, scalars=sc,
            scratch=[pltpu.VMEM((width, joint_width), bf16)],
        )
        kv_theirs = swap_col(kv_mine)
        q, k, v, probs, heads, part, send = call(
            attn_body,
            [((t, qw), bf16), ((t, hd), bf16), ((t, hd), bf16), ((n_head, t, t), f32),
             ((t, qw), bf16), wide_f, wide_b],
            raw_q, kv_mine, kv_theirs, mask, cos, sin, gq, gk, *wo, scalars=sc,
            scratch=[pltpu.VMEM((width, qw), bf16)],
        )
        (cotangent,) = call(cot_body, [wide_f], *cot_pieces, scalars=sc)
        proj, mid, ffn_in, gate, up, hidden = call(
            mix_body,
            [wide_f, wide_f, wide_b, ((t, ff), f32), ((t, ff), f32), ((t, ff), bf16)],
            x, part, swap_col(send), gains, *wg, *wu, scalars=sc,
            scratch=ffn_scratch[:2],
        )
        part, send = call(
            down_body, [wide_f, wide_b], hidden, *wd, scalars=sc,
            scratch=ffn_scratch[:1],
        )

        def first_shapes(name, n):
            s = stage_shapes(2, half_width, n, PLAN[name][0])
            return [(s, bf16), (s, f32)]

        def swap(v, d):
            return swap_row(v) if d == "y" else swap_dp(v, d)

        def more_bits(cur):
            n = cur.shape[-1]
            for bit in extra:
                size = cur.shape[1] // 2
                halves = cur.reshape(2, size, n).astype(f32)
                b = bit_of(bit)
                sent = lax.dynamic_index_in_dim(halves, 1 - b, 0).astype(bf16)
                got = swap_dp(sent, bit).astype(f32)
                cur = lax.dynamic_index_in_dim(halves, b, 0) + got
            cur = cur.astype(bf16)
            for bit in reversed(extra):
                theirs = swap_dp(cur, bit)
                b = bit_of(bit)
                cur = jnp.concatenate(
                    [jnp.where(b == 0, cur, theirs), jnp.where(b == 0, theirs, cur)], axis=1
                )
            return cur

        def grad_sum(name, send, keep, outs):
            n = keep.shape[-1]
            order = PLAN[name]
            left = list(TOP_BITS)
            if order[0] != "y":
                left.remove(order[0])
            for stage, d in enumerate(order):
                recv = swap(send, d)
                if stage + 1 == len(order):
                    break
                nxt = order[stage + 1]
                blocks, r, _ = keep.shape
                shape = stage_shapes(blocks, r, n, nxt)
                send, keep = call(
                    stage_body(nxt, tuple(left)),
                    [(shape, bf16), (shape, f32)], keep, recv, scalars=sc,
                    scratch=[pltpu.VMEM((blocks, r, n), f32)],
                )
                if nxt != "y":
                    left.remove(nxt)
            (cur,) = call(last_sum_body, [(keep.shape, bf16)], keep, recv)
            if extra:
                cur = more_bits(cur)
            stage = len(order) - 1
            for d in GATHER[name]:
                stage += 1
                theirs = swap_dp(cur, d)
                if d != GATHER[name][-1]:
                    cur = jnp.concatenate([cur, theirs], axis=0)
            return call(
                assemble_body(GATHER[name], [w for w, _ in outs]),
                [((half_width, w), dt) for w, dt in outs], cur, theirs, scalars=sc, out_hbm=True,
            )

        def place_out(own_t, send):
            return jnp.where(diag, own_t, diag_to_off_row(send).astype(f32)).T

        out_pair = [((half_width, t), f32), ((half_width, t), bf16)]
        own_t, out_send, grad_ffn, post_part, s_down, k_down = call(
            down_grad_body,
            out_pair + [wide_b, ((1, width), f32)] + first_shapes("down", ff),
            mid, part, swap_col(send), cotangent, gains, hidden, scalars=sc,
        )
        block_output = place_out(own_t, out_send)
        (down_sum,) = grad_sum("down", s_down, k_down, [(ff, f32)])
        s_gate, k_gate, s_up, k_up, part, send = call(
            mix_grad_body,
            first_shapes("gate", ff) + first_shapes("up", ff) + [wide_f, wide_b],
            grad_ffn, gate, up, ffn_in, *wg, *wu, *wd, scalars=sc,
            scratch=ffn_scratch + [pltpu.VMEM((2, half_width, ff), f32)],
        )
        (gate_sum,) = grad_sum("gate", s_gate, k_gate, [(ff, f32)])
        (up_sum,) = grad_sum("up", s_up, k_up, [(ff, f32)])
        grad_mid, grad_attn, pre_part, attn_part, kv_own, kv_send, grad_q, q_part = call(
            attn_grad_body,
            [wide_f, wide_b, ((1, width), f32), ((1, width), f32),
             ((t, hd), f32), ((t, hd), f32), ((t, qw), bf16), ((1, hd), f32)],
            part, swap_col(send), mid, proj, cotangent, gains, *wo, q, k, v, probs,
            raw_q, cos, sin, gq, scalars=sc, scratch=[pltpu.VMEM((width, qw), bf16)],
        )
        n_attn = joint_width + qw
        k_part, s_attn, k_attn, part, send = call(
            joint_body,
            [((1, hd), f32)] + first_shapes("attn", n_attn) + [wide_f, wide_b],
            kv_own, swap_col(kv_send), kv_mine, cos, sin, gk, grad_q, normed,
            grad_attn, heads, *w_joint, scalars=sc,
            scratch=[pltpu.VMEM((width, joint_width), bf16),
                     pltpu.VMEM((2, half_width, n_attn), f32)],
        )
        query_sum, kv_sum, out_sum = grad_sum(
            "attn", s_attn, k_attn, [(qw, f32), (hd, bf16), (qw, f32)]
        )
        own_t, out_send, in_part = call(
            input_body, out_pair + [((1, width), f32)],
            part, swap_col(send), x, grad_mid, gains,
        )
        input_grad = place_out(own_t, out_send)
        kv_sum_theirs = swap_col(kv_sum)
        key_sum = jnp.where(first_col, kv_sum, kv_sum_theirs).astype(f32)
        value_sum = jnp.where(first_col, kv_sum_theirs, kv_sum).astype(f32)

        width_parts = jnp.concatenate([in_part, attn_part, pre_part, post_part], axis=0)
        width_parts = jnp.where(diag, width_parts, 0.0)
        ends = [q_part[0], k_part[0]]
        own = jnp.concatenate([width_parts[:, :half_width].reshape(-1)] + ends)
        away = jnp.concatenate([width_parts[:, half_width:].reshape(-1)] + ends)
        small = own + swap_row(away)
        small = small + swap_col(small)
        for bit in bits:
            small = small + swap_dp(small, bit)
        width_sums = small[: 4 * half_width].reshape(4, half_width)
        return (
            block_output, input_grad, query_sum, key_sum, value_sum, out_sum.T,
            gate_sum, up_sum, down_sum.T,
            width_sums[0], width_sums[1], width_sums[2], width_sums[3],
            small[4 * half_width : 4 * half_width + hd], small[4 * half_width + hd :],
        )

    return step


def solution(mesh):
    rows_by_width = P(("dp", "col"), "row")
    in_specs = (
        rows_by_width, P(("dp", "row"), None), P("row", "col"), P("row", None), P("row", None),
        P("col", "row"), P("row", "col"), P("row", "col"), P("col", "row"),
        P("row"), P("row"), P("row"), P("row"), P(), P(), rows_by_width,
    )
    out_specs = (
        rows_by_width, rows_by_width, P("row", "col"), P("row", None), P("row", None),
        P("col", "row"), P("row", "col"), P("row", "col"), P("col", "row"),
        P("row"), P("row"), P("row"), P("row"), P(), P(),
    )
    return jax.shard_map(
        make_step(mesh), mesh=mesh, in_specs=in_specs, out_specs=out_specs, check_vma=False
    )
```

```python
import jax
import jax.numpy as jnp
from jax import lax
from jax.experimental import pallas as pl
from jax.experimental.pallas import tpu as pltpu
from jax.sharding import PartitionSpec as P

eps_norm = 1e-06
rope_base = 1000000.0
bf16 = jnp.bfloat16
f32 = jnp.float32
gelu_c = (2.0 / 3.141592653589793) ** 0.5
gelu_a = 0.044715
gain_cols = 128


PLAN = {
    "down": (2, 1, "y", 4),
    "gate": (1, 2, "y", 4),
    "up": (2, 1, "y", 4),
    "attn": ("y", 1, 2, 4),
}
GATHER = {"down": (2, 1), "gate": (2, 1), "up": (2, 1), "attn": (1, 2)}
TOP_BITS = (1, 2, 4)


def dot(left, right, contract=((1,), (0,))):
    return lax.dot_general(left, right, (contract, ((), ())), preferred_element_type=f32)


def rms_scale(values):
    return lax.rsqrt(jnp.mean(values * values, axis=-1, keepdims=True) + eps_norm)


def norm_back(upstream, values, inv_rms, gain_vector):
    weighted = upstream * gain_vector
    width_sum = jnp.sum(weighted * values, axis=1, keepdims=True)
    through = inv_rms * weighted - values * (inv_rms**3 * width_sum / values.shape[1])
    return through, jnp.sum(upstream * values * inv_rms, axis=0, keepdims=True)


def rotate(values, cosine_table, sine_table):
    half = values.shape[1] // 2
    a, b = values[:, :half], values[:, half:]
    return jnp.concatenate(
        [a * cosine_table - b * sine_table, b * cosine_table + a * sine_table], axis=1
    )


def rotate_back(values, cosine_table, sine_table):
    return rotate(values, cosine_table, -sine_table)


def gelu_parts(v):
    t = jnp.tanh(gelu_c * (v + gelu_a * v * v * v))
    return t, 0.5 * v * (1.0 + t)


def call(body, outs, *args, scalars=None, scratch=(), out_hbm=False, limit=24):
    in_specs = [pl.BlockSpec(memory_space=pltpu.VMEM) for _ in args]
    args = tuple(pltpu.with_memory_space_constraint(v, pltpu.VMEM) for v in args)
    if scalars is not None:
        in_specs = [pl.BlockSpec(memory_space=pltpu.SMEM)] + in_specs
        args = (scalars,) + args
    place = jax.ShapeDtypeStruct if out_hbm else pltpu.VMEM
    return pl.pallas_call(
        body,
        in_specs=in_specs,
        out_specs=[pl.BlockSpec(memory_space=pltpu.VMEM) for _ in outs],
        out_shape=[place(s, d) for s, d in outs],
        scratch_shapes=list(scratch),
        compiler_params=pltpu.CompilerParams(vmem_limit_bytes=limit << 20),
    )(*args)


def join_rows(scr, own, other):
    half = own.shape[0]
    scr[:half, :] = own[...]
    scr[half:, :] = other[...]


def place_rows(scr, sc, own, group, first_bit, source, target):
    near, first, second = group
    half, q = own.shape[0], near.shape[0]
    scr[:half, target] = own[:, target]
    b1, b2 = sc[1], sc[2]

    def at(r1, r2):
        p1 = 1 - b1 if r1 else b1
        p2 = 1 - b2 if r2 else b2
        return pl.ds(pl.multiple_of(half + q * (2 * p2 + p1), 16), q)

    scr[at(0, 0), target] = near[:, source]
    scr[at(1, 0) if first_bit == 1 else at(0, 1), target] = first[:, source]
    scr[at(0, 1) if first_bit == 1 else at(1, 0), target] = second[:q, source]
    scr[at(1, 1), target] = second[q:, source]


def place_mix(wg, wu, sc, own_g, own_u, e1, e2):
    ff = wg.shape[1]
    place_rows(wg, sc, own_g, e1, 1, slice(0, ff), slice(0, ff))
    place_rows(wu, sc, own_u, e2, 2, slice(0, ff), slice(0, ff))


def place_down(wd, sc, own, e1, e2):
    ff = wd.shape[1]
    tail = slice(ff, ff + ff // 2)
    place_rows(wd, sc, own, e1, 1, tail, slice(0, ff // 2))
    place_rows(wd, sc, own, e2, 2, tail, slice(ff // 2, ff))


def sequence_t(sc, local, own_recv, diag_recv, other_recv):
    diag = sc[3] == 1
    own = jnp.where(diag, local[...], own_recv[...].astype(f32))
    other = jnp.where(diag, diag_recv[...].astype(f32), other_recv[...].astype(f32))
    return jnp.concatenate([own, other], axis=0).T


def proj_body(sc, x_local, x_own, x_diag, x_other, g, w_own, w_other, x, normed, raw_q, kv, w):
    join_rows(w, w_own, w_other)
    v = sequence_t(sc, x_local, x_own, x_diag, x_other)
    x[...] = v
    n = (v * rms_scale(v) * g[0:1, :]).astype(bf16)
    normed[...] = n
    p = dot(n, w[...])
    qw = raw_q.shape[1]
    raw_q[...] = p[:, :qw]
    kv[...] = p[:, qw:]


def cot_body(sc, c_local, c_diag, c_off, cot):
    here = jnp.concatenate([c_local[...], c_diag[...].astype(f32)], axis=0)
    cot[...] = jnp.where(sc[3] == 1, here, c_off[...].astype(f32)).T


def attn_body(sc, raw_q, kv_mine, kv_theirs, mask, cos, sin, gq, gk, w_own, w_other, q, k, v,
              probs, heads, part, send, w):
    join_rows(w, w_own, w_other)
    first = sc[0] == 1
    c, s = cos[...], sin[...]
    hd = k.shape[1]
    raw_k = jnp.where(first, kv_mine[...], kv_theirs[...])
    raw_v = jnp.where(first, kv_theirs[...], kv_mine[...])
    key = rotate(raw_k * rms_scale(raw_k) * gk[...], c, s).astype(bf16)
    value = raw_v.astype(bf16)
    k[...] = key
    v[...] = value
    allowed = mask[...] > 0.0
    for h in range(q.shape[1] // hd):
        raw = raw_q[:, h * hd : (h + 1) * hd]
        query = rotate(raw * rms_scale(raw) * gq[...], c, s).astype(bf16)
        q[:, h * hd : (h + 1) * hd] = query
        logits = dot(query, key, ((1,), (1,))) * (hd**-0.5)
        weights = jnp.where(allowed, jnp.exp(logits), 0.0)
        p = weights / jnp.sum(weights, axis=1, keepdims=True)
        probs[h] = p
        heads[:, h * hd : (h + 1) * hd] = dot(p.astype(bf16), value).astype(bf16)
    out = dot(heads[...], w[...], ((1,), (1,)))
    part[...] = out
    send[...] = out.astype(bf16)


def mix_body(sc, x, own, recv, g, *refs):
    proj, mid, ffn_in, gate, up, hidden, wg, wu = refs[8:]
    place_mix(wg, wu, sc, refs[0], refs[1], refs[2:5], refs[5:8])
    y = own[...] + recv[...].astype(f32)
    proj[...] = y
    m = x[...] + y * rms_scale(y) * g[1:2, :]
    mid[...] = m
    n = (m * rms_scale(m) * g[2:3, :]).astype(bf16)
    ffn_in[...] = n
    ga = dot(n, wg[...])
    gate[...] = ga
    u = dot(n, wu[...])
    up[...] = u
    hidden[...] = (gelu_parts(ga)[1] * u).astype(bf16)


def down_body(sc, hidden, *refs):
    part, send, wd = refs[7:]
    place_down(wd, sc, refs[0], refs[1:4], refs[4:7])
    out = dot(hidden[...], wd[...], ((1,), (1,)))
    part[...] = out
    send[...] = out.astype(bf16)


def split_axis(sc, src, blocks, rows, left, d, emit):
    if d == "y":
        emit(0, 0, src(0, 0, rows), src(1, 0, rows))
        return
    groups = 1 << left.index(d)
    size = rows // groups
    half = size // 2
    b = sc[{1: 1, 2: 2, 4: 4}[d]]
    for block in range(blocks):
        for i in range(groups):
            mine = pl.multiple_of(i * size + b * half, 8)
            theirs = pl.multiple_of(i * size + (1 - b) * half, 8)
            emit(block, i * half, src(block, mine, half), src(block, theirs, half))


def split_grad(sc, left_t, right, send, keep, acc, d, col=0):
    split_sum(sc, dot(left_t, right), send, keep, acc, d, col)


def split_sum(sc, g, send, keep, acc, d, col=0):
    n = g.shape[1]
    cols = slice(col, col + n)
    half = g.shape[0] // 2
    if d == "y":
        send[0, :, cols] = g[half:].astype(bf16)
        keep[0, :, cols] = g[:half]
        return
    acc[0, :, cols] = g[:half]
    acc[1, :, cols] = g[half:]

    def emit(block, at, mine, theirs):
        rows = slice(at, at + mine.shape[0])
        send[block, rows, cols] = theirs.astype(bf16)
        keep[block, rows, cols] = mine

    split_axis(
        sc, lambda block, start, size: acc[block, pl.ds(start, size), cols], 2, half, TOP_BITS,
        d, emit,
    )


def stage_shapes(blocks, rows, n, d):
    if d == "y":
        return (1, rows, n)
    return (blocks, rows // 2, n)


def stage_body(d, left):
    def body(sc, keep_in, recv, send, keep, acc):
        blocks, rows, _ = keep_in.shape
        for block in range(blocks):
            acc[block] = keep_in[block] + recv[block].astype(f32)

        def emit(block, at, mine, theirs):
            span = slice(at, at + mine.shape[0])
            send[block, span, :] = theirs.astype(bf16)
            keep[block, span, :] = mine

        split_axis(
            sc, lambda block, start, size: acc[block, pl.ds(start, size), :], blocks, rows, left,
            d, emit,
        )

    return body


def last_sum_body(keep_in, recv, send):
    send[...] = (keep_in[...].astype(f32) + recv[...].astype(f32)).astype(bf16)


def assemble_body(order, widths):
    def body(sc, near, far, *outs):
        rows = near.shape[1]
        for part, ref in ((0, near), (1, far)):
            for j in range(2):
                rel = {order[0]: j, order[1]: part}
                p1 = 1 - sc[1] if rel[1] else sc[1]
                p2 = 1 - sc[2] if rel[2] else sc[2]
                at = pl.ds(pl.multiple_of((2 * p1 + p2) * rows, 8), rows)
                val = ref[j].astype(f32)
                col = 0
                for out, w in zip(outs, widths):
                    out[at, :] = val[:, col : col + w].astype(out.dtype)
                    col += w

    return body


def down_grad_body(sc, mid, own, recv, cot, g, hidden, out, out_send, grad_ffn, gain_part, send,
                   keep, acc):
    f = own[...] + recv[...].astype(f32)
    s = rms_scale(f)
    full = (mid[...] + f * s * g[3:4, :]).T
    half = full.shape[0] // 2
    out[...] = full[:half]
    out_send[...] = full[half:].astype(bf16)
    through, part = norm_back(cot[...], f, s, g[3:4, :])
    gain_part[...] = part
    gf = through.astype(bf16)
    grad_ffn[...] = gf
    split_grad(sc, gf.T, hidden[...], send, keep, acc, PLAN["down"][0])


def mix_grad_body(sc, grad_ffn, gate, up, ffn_in, *refs):
    s_gate, k_gate, s_up, k_up, part, send, wg, wu, wd, acc = refs[9:]
    place_down(wd, sc, refs[2], refs[3:6], refs[6:9])
    place_mix(wg, wu, sc, refs[0], refs[1], refs[3:6], refs[6:9])
    gh = dot(grad_ffn[...], wd[...])
    v = gate[...]
    t, gelu = gelu_parts(v)
    slope = 0.5 * (1.0 + t) + 0.5 * v * (1.0 - t * t) * (gelu_c * (1.0 + 3.0 * gelu_a * v * v))
    gg = (gh * up[...] * slope).astype(bf16)
    gu = (gh * gelu).astype(bf16)
    n_t = ffn_in[...].T
    split_grad(sc, n_t, gg, s_gate, k_gate, acc, PLAN["gate"][0])
    split_grad(sc, n_t, gu, s_up, k_up, acc, PLAN["up"][0])
    out = dot(gg, wg[...], ((1,), (1,))) + dot(gu, wu[...], ((1,), (1,)))
    part[...] = out
    send[...] = out.astype(bf16)


def attn_grad_body(sc, own, recv, mid, proj, cot, g, w_own, w_other, q, k, v, probs, raw_q, cos,
                   sin, gq, grad_mid, grad_attn, pre_part, attn_part, kv_own, kv_send, grad_q,
                   q_part, w):
    join_rows(w, w_own, w_other)
    up = own[...] + recv[...].astype(f32)
    m = mid[...]
    through, part = norm_back(up, m, rms_scale(m), g[2:3, :])
    pre_part[...] = part
    gm = cot[...] + through
    grad_mid[...] = gm
    y = proj[...]
    through, part = norm_back(gm, y, rms_scale(y), g[1:2, :])
    attn_part[...] = part
    ga = through.astype(bf16)
    grad_attn[...] = ga
    grad_heads = dot(ga, w[...]).astype(bf16)
    hd = k.shape[1]
    c, s = cos[...], sin[...]
    key, value = k[...], v[...]
    value_part, key_part, gain_part = 0.0, 0.0, 0.0
    scale = hd**-0.5
    for h in range(q.shape[1] // hd):
        cols = slice(h * hd, (h + 1) * hd)
        gh = grad_heads[:, cols]
        p = probs[h]
        value_part = value_part + dot(p.astype(bf16).T, gh)
        gp = dot(gh, value, ((1,), (1,)))
        delta = jnp.sum(p * gp, axis=1, keepdims=True)
        gs = (p * (gp - delta)).astype(bf16)
        gq_rot = dot(gs, key) * scale
        key_part = key_part + dot(gs.T, q[:, cols]) * scale
        raw = raw_q[:, cols]
        through, part = norm_back(rotate_back(gq_rot, c, s), raw, rms_scale(raw), gq[...])
        grad_q[:, cols] = through.astype(bf16)
        gain_part = gain_part + part
    q_part[...] = gain_part
    first = sc[0] == 1
    kv_own[...] = jnp.where(first, key_part, value_part)
    kv_send[...] = jnp.where(first, value_part, key_part)


def joint_body(sc, kv_own, kv_recv, kv_raw, cos, sin, gk, grad_q, normed, grad_attn, heads, x,
               attn_part, pre_part, post_part, q_part, w_own, w_other, send, keep, part,
               part_send, w, acc):
    join_rows(w, w_own, w_other)
    total = kv_own[...] + kv_recv[...]
    raw = kv_raw[...]
    through, gain_part = norm_back(
        rotate_back(total, cos[...], sin[...]), raw, rms_scale(raw), gk[...]
    )
    first = sc[0] == 1
    k_part = jnp.where(first, gain_part, 0.0)
    kvg = jnp.where(first, through, total).astype(bf16)
    gq = grad_q[...]
    qw, kw = gq.shape[1], kvg.shape[1]
    n_t = normed[...].T
    d = PLAN["attn"][0]
    split_grad(sc, n_t, gq, send, keep, acc, d, 0)
    split_grad(sc, n_t, kvg, send, keep, acc, d, qw)
    out = dot(gq, w[:, :qw], ((1,), (1,))) + dot(kvg, w[:, qw:], ((1,), (1,)))
    part[...] = out
    part_send[...] = out.astype(bf16)
    v = x[...]
    in_part = jnp.sum(out * v * rms_scale(v), axis=0, keepdims=True)
    diag = sc[3] == 1
    shared = [jnp.where(diag, ref[...], 0.0) for ref in (attn_part, pre_part, post_part)]
    half = v.shape[1] // 2
    wide = jnp.concatenate(
        [in_part] + shared + [jnp.zeros((gain_cols - 4, v.shape[1]), f32)], axis=0
    ).T
    ends = jnp.concatenate(
        [jnp.zeros((4, kw), f32), q_part[...], k_part, jnp.zeros((gain_cols - 6, kw), f32)],
        axis=0,
    ).T
    ends = jnp.concatenate([ends, jnp.zeros((half - kw, gain_cols), f32)], axis=0)
    gains = wide + jnp.concatenate([ends, ends], axis=0)
    split_sum(sc, gains, send, keep, acc, d, qw + kw)
    split_grad(sc, grad_attn[...].T, heads[...], send, keep, acc, d, qw + kw + gain_cols)


def finish_body(sc, own, recv, key, value, gains):
    first = sc[0] == 1
    kw = key.shape[1]
    a, b = own[:, :kw].astype(f32), recv[:, :kw].astype(f32)
    key[...] = jnp.where(first, a, b)
    value[...] = jnp.where(first, b, a)
    gains[...] = (own[:, kw:].astype(f32) + recv[:, kw:].astype(f32)).T[: gains.shape[0]]


def input_body(own, recv, x, grad_mid, g, out, out_send):
    up = own[...] + recv[...].astype(f32)
    v = x[...]
    through, _ = norm_back(up, v, rms_scale(v), g[0:1, :])
    full = (grad_mid[...] + through).T
    half = full.shape[0] // 2
    out[...] = full[:half]
    out_send[...] = full[half:].astype(bf16)


def make_step(mesh):
    n_dp, n_row, n_col = mesh.shape["dp"], mesh.shape["row"], mesh.shape["col"]
    assert n_row == 2 and n_col == 2 and n_dp >= 8
    bits = []
    while (1 << len(bits)) < n_dp:
        bits.append(1 << len(bits))
    assert (1 << len(bits)) == n_dp
    extra = tuple(b for b in bits if b > 4)

    def swap_row(v):
        return lax.ppermute(v, "row", [(0, 1), (1, 0)])

    def swap_col(v):
        return lax.ppermute(v, "col", [(0, 1), (1, 0)])

    def swap_dp(v, bit):
        return lax.ppermute(v, "dp", [(i, i ^ bit) for i in range(n_dp)])

    def step(
        block_input, segment_ids, w_query, w_key, w_value, w_out, w_gate, w_up, w_down,
        gain_input, gain_attn, gain_ffn_pre, gain_ffn_post, gain_query, gain_key, out_cotangent,
    ):
        rows, half_width = block_input.shape
        width = 2 * half_width
        hd = w_key.shape[1]
        qw = w_query.shape[1]
        n_head = qw // hd
        ff = w_gate.shape[1]
        row = lax.axis_index("row")
        col = lax.axis_index("col")
        dp = lax.axis_index("dp")
        diag = row == col
        first_col = col == 0

        def bit_of(bit):
            return (dp // bit) % 2

        code = (1 - col) + 2 * bit_of(1) + 4 * bit_of(2) + 8 * (row == col) + 16 * bit_of(4)
        sc = (code >> jnp.arange(8, dtype=jnp.int32)) & 1

        def off_to_diag(v):
            return lax.ppermute(v, ("row", "col"), [(1, 3), (2, 0)])

        def diag_to_off_col(v):
            return lax.ppermute(v, ("row", "col"), [(0, 1), (3, 2)])

        def diag_to_off_row(v):
            return lax.ppermute(v, ("row", "col"), [(0, 2), (3, 1)])

        def chip_sequence(local, kind):
            local_t = local.T
            narrow = local_t.astype(kind)
            from_row = off_to_diag(narrow)
            return local_t, diag_to_off_col(narrow), from_row, diag_to_off_col(from_row)

        def other_rows(own, first_bit, second_bit):
            q = half_width // 4
            at = (2 * bit_of(2) + bit_of(1)) * q
            part = jnp.concatenate([lax.dynamic_slice_in_dim(w, at, q, 0) for w in own], axis=1)
            near = swap_row(part)
            first = swap_dp(near, first_bit)
            second = swap_dp(jnp.concatenate([near, first], axis=0), second_bit)
            return near, first, second

        x_pieces = chip_sequence(block_input, f32)
        joint_own = jnp.concatenate([w_query, jnp.where(first_col, w_key, w_value)], axis=1)
        w_joint = (joint_own, swap_row(joint_own))
        which = lax.broadcasted_iota(jnp.int32, (4, half_width), 0)
        gains_own = jnp.where(
            which == 0, gain_input,
            jnp.where(which == 1, gain_attn, jnp.where(which == 2, gain_ffn_pre, gain_ffn_post)),
        )
        gains = jnp.concatenate([gains_own, swap_row(gains_own)], axis=1)
        out_own = w_out.T
        wo = (out_own, swap_row(out_own))
        down_own = w_down.T
        e1 = other_rows((w_gate, down_own[:, : ff // 2]), 1, 2)
        e2 = other_rows((w_up, down_own[:, ff // 2 :]), 2, 1)
        cot_t = out_cotangent.T
        cot_narrow = cot_t.astype(bf16)
        cot_diag = off_to_diag(cot_narrow)
        cot_off = diag_to_off_col(jnp.concatenate([cot_narrow, cot_diag], axis=0))

        segments = segment_ids[0]
        places = jnp.arange(rows, dtype=jnp.int32)
        allowed = (segments[:, None] == segments[None, :]) & (places[:, None] >= places[None, :])
        mask = allowed.astype(f32)
        offsets = jnp.sum(mask, axis=1) - 1.0
        frequency = rope_base ** (-(jnp.arange(hd // 2, dtype=f32) * 2.0 / hd))
        angles = offsets[:, None] * frequency
        cos, sin = jnp.cos(angles), jnp.sin(angles)
        gq, gk = gain_query[None], gain_key[None]

        t = rows
        joint_width = qw + hd
        wide_f, wide_b = ((t, width), f32), ((t, width), bf16)
        ffn_scratch = [pltpu.VMEM((width, ff), bf16) for _ in range(3)]
        x, normed, raw_q, kv_mine = call(
            proj_body, [wide_f, wide_b, ((t, qw), f32), ((t, hd), f32)],
            *x_pieces, gains, *w_joint, scalars=sc,
            scratch=[pltpu.VMEM((width, joint_width), bf16)],
        )
        kv_theirs = swap_col(kv_mine)
        q, k, v, probs, heads, part, send = call(
            attn_body,
            [((t, qw), bf16), ((t, hd), bf16), ((t, hd), bf16), ((n_head, t, t), f32),
             ((t, qw), bf16), wide_f, wide_b],
            raw_q, kv_mine, kv_theirs, mask, cos, sin, gq, gk, *wo, scalars=sc,
            scratch=[pltpu.VMEM((width, qw), bf16)],
        )
        (cotangent,) = call(cot_body, [wide_f], cot_t, cot_diag, cot_off, scalars=sc)
        proj, mid, ffn_in, gate, up, hidden = call(
            mix_body,
            [wide_f, wide_f, wide_b, ((t, ff), f32), ((t, ff), f32), ((t, ff), bf16)],
            x, part, swap_col(send), gains, w_gate, w_up, *e1, *e2, scalars=sc,
            scratch=ffn_scratch[:2],
        )
        part, send = call(
            down_body, [wide_f, wide_b], hidden, down_own, *e1, *e2, scalars=sc,
            scratch=ffn_scratch[:1],
        )

        def first_shapes(name, n):
            s = stage_shapes(2, half_width, n, PLAN[name][0])
            return [(s, bf16), (s, f32)]

        def swap(v, d):
            return swap_row(v) if d == "y" else swap_dp(v, d)

        def more_bits(cur):
            n = cur.shape[-1]
            for bit in extra:
                size = cur.shape[1] // 2
                halves = cur.reshape(2, size, n).astype(f32)
                b = bit_of(bit)
                sent = lax.dynamic_index_in_dim(halves, 1 - b, 0).astype(bf16)
                got = swap_dp(sent, bit).astype(f32)
                cur = lax.dynamic_index_in_dim(halves, b, 0) + got
            cur = cur.astype(bf16)
            for bit in reversed(extra):
                theirs = swap_dp(cur, bit)
                b = bit_of(bit)
                cur = jnp.concatenate(
                    [jnp.where(b == 0, cur, theirs), jnp.where(b == 0, theirs, cur)], axis=1
                )
            return cur

        def grad_sum(name, send, keep, outs):
            n = keep.shape[-1]
            order = PLAN[name]
            left = list(TOP_BITS)
            if order[0] != "y":
                left.remove(order[0])
            for stage, d in enumerate(order[:-1]):
                recv = swap(send, d)
                if stage == len(order) - 2:
                    break
                nxt = order[stage + 1]
                blocks, r, _ = keep.shape
                shape = stage_shapes(blocks, r, n, nxt)
                send, keep = call(
                    stage_body(nxt, tuple(left)),
                    [(shape, bf16), (shape, f32)], keep, recv, scalars=sc,
                    scratch=[pltpu.VMEM((blocks, r, n), f32)],
                )
                if nxt != "y":
                    left.remove(nxt)
            (cur,) = call(last_sum_body, [(keep.shape, bf16)], keep, recv)
            stage = len(order) - 1
            recv = swap_dp(cur, order[-1])
            (cur,) = call(last_sum_body, [(cur.shape, bf16)], cur, recv)
            if extra:
                cur = more_bits(cur)
            for d in GATHER[name]:
                stage += 1
                theirs = swap_dp(cur, d)
                if d != GATHER[name][-1]:
                    cur = jnp.concatenate([cur, theirs], axis=0)
            return call(
                assemble_body(GATHER[name], [w for w, _ in outs]),
                [((half_width, w), dt) for w, dt in outs], cur, theirs, scalars=sc, out_hbm=True,
            )

        out_pair = [((half_width, t), f32), ((half_width, t), bf16)]
        out_own_t, out_send, grad_ffn, post_part, s_down, k_down = call(
            down_grad_body,
            out_pair + [wide_b, ((1, width), f32)] + first_shapes("down", ff),
            mid, part, swap_col(send), cotangent, gains, hidden, scalars=sc,
            scratch=[pltpu.VMEM((2, half_width, ff), f32)],
        )
        (down_sum,) = grad_sum("down", s_down, k_down, [(ff, f32)])
        s_gate, k_gate, s_up, k_up, part, send = call(
            mix_grad_body,
            first_shapes("gate", ff) + first_shapes("up", ff) + [wide_f, wide_b],
            grad_ffn, gate, up, ffn_in, w_gate, w_up, down_own, *e1, *e2, scalars=sc,
            scratch=ffn_scratch + [pltpu.VMEM((2, half_width, ff), f32)],
        )
        (gate_sum,) = grad_sum("gate", s_gate, k_gate, [(ff, f32)])
        (up_sum,) = grad_sum("up", s_up, k_up, [(ff, f32)])
        grad_mid, grad_attn, pre_part, attn_part, kv_own, kv_send, grad_q, q_part = call(
            attn_grad_body,
            [wide_f, wide_b, ((1, width), f32), ((1, width), f32),
             ((t, hd), f32), ((t, hd), f32), ((t, qw), bf16), ((1, hd), f32)],
            part, swap_col(send), mid, proj, cotangent, gains, *wo, q, k, v, probs,
            raw_q, cos, sin, gq, scalars=sc, scratch=[pltpu.VMEM((width, qw), bf16)],
        )
        n_attn = joint_width + gain_cols + qw
        s_attn, k_attn, part, send = call(
            joint_body, first_shapes("attn", n_attn) + [wide_f, wide_b],
            kv_own, swap_col(kv_send), kv_mine, cos, sin, gk, grad_q, normed,
            grad_attn, heads, x, attn_part, pre_part, post_part, q_part, *w_joint, scalars=sc,
            scratch=[pltpu.VMEM((width, joint_width), bf16),
                     pltpu.VMEM((2, half_width, n_attn), f32)],
        )
        query_sum, kv_sum, out_sum = grad_sum(
            "attn", s_attn, k_attn, [(qw, f32), (hd + gain_cols, bf16), (qw, f32)]
        )
        in_own_t, in_send = call(
            input_body, out_pair,
            part, swap_col(send), x, grad_mid, gains,
        )
        both = diag_to_off_row(jnp.concatenate([out_send, in_send], axis=0)).astype(f32)
        block_output = jnp.where(diag, out_own_t, both[:half_width]).T
        input_grad = jnp.where(diag, in_own_t, both[half_width:]).T
        key_sum, value_sum, gain_sum = call(
            finish_body,
            [((half_width, hd), f32), ((half_width, hd), f32), ((8, half_width), f32)],
            kv_sum, swap_col(kv_sum), scalars=sc, out_hbm=True,
        )
        return (
            block_output, input_grad, query_sum, key_sum, value_sum, out_sum.T,
            gate_sum, up_sum, down_sum.T,
            gain_sum[0], gain_sum[1], gain_sum[2], gain_sum[3],
            gain_sum[4, :hd], gain_sum[5, :hd],
        )

    return step


def solution(mesh):
    rows_by_width = P(("dp", "col"), "row")
    in_specs = (
        rows_by_width, P(("dp", "row"), None), P("row", "col"), P("row", None), P("row", None),
        P("col", "row"), P("row", "col"), P("row", "col"), P("col", "row"),
        P("row"), P("row"), P("row"), P("row"), P(), P(), rows_by_width,
    )
    out_specs = (
        rows_by_width, rows_by_width, P("row", "col"), P("row", None), P("row", None),
        P("col", "row"), P("row", "col"), P("row", "col"), P("col", "row"),
        P("row"), P("row"), P("row"), P("row"), P(), P(),
    )
    return jax.shard_map(
        make_step(mesh), mesh=mesh, in_specs=in_specs, out_specs=out_specs, check_vma=False
    )
```

```python
import jax
import jax.numpy as jnp
from jax import lax
from jax.experimental import pallas as pl
from jax.experimental.pallas import tpu as pltpu
from jax.sharding import PartitionSpec as P

eps_norm = 1e-06
rope_base = 1000000.0
bf16 = jnp.bfloat16
f32 = jnp.float32
gelu_c = (2.0 / 3.141592653589793) ** 0.5
gelu_a = 0.044715
gain_cols = 128


PLAN = {
    "down": ("y", 2, 1, 4),
    "gate": (2, 1, "y", 4),
    "up": (1, 2, "y", 4),
    "out": ("y", 2, 1, 4),
    "qkv": ("y", 2, 1, 4),
}
GATHER = {"down": (2, 1), "gate": (1, 2), "up": (2, 1), "out": (2, 1), "qkv": (1, 2)}
TOP_BITS = (1, 2, 4)


def dot(left, right, contract=((1,), (0,))):
    return lax.dot_general(left, right, (contract, ((), ())), preferred_element_type=f32)


def rms_scale(values):
    return lax.rsqrt(jnp.mean(values * values, axis=-1, keepdims=True) + eps_norm)


def norm_back(upstream, values, inv_rms, gain_vector):
    weighted = upstream * gain_vector
    width_sum = jnp.sum(weighted * values, axis=1, keepdims=True)
    through = inv_rms * weighted - values * (inv_rms**3 * width_sum / values.shape[1])
    return through, jnp.sum(upstream * values * inv_rms, axis=0, keepdims=True)


def rotate(values, cosine_table, sine_table):
    half = values.shape[1] // 2
    a, b = values[:, :half], values[:, half:]
    return jnp.concatenate(
        [a * cosine_table - b * sine_table, b * cosine_table + a * sine_table], axis=1
    )


def rotate_back(values, cosine_table, sine_table):
    return rotate(values, cosine_table, -sine_table)


def gelu_parts(v):
    t = jnp.tanh(gelu_c * (v + gelu_a * v * v * v))
    return t, 0.5 * v * (1.0 + t)


def call(body, outs, *args, scalars=None, scratch=(), out_hbm=False, limit=24):
    in_specs = [pl.BlockSpec(memory_space=pltpu.VMEM) for _ in args]
    args = tuple(pltpu.with_memory_space_constraint(v, pltpu.VMEM) for v in args)
    if scalars is not None:
        in_specs = [pl.BlockSpec(memory_space=pltpu.SMEM)] + in_specs
        args = (scalars,) + args
    place = jax.ShapeDtypeStruct if out_hbm else pltpu.VMEM
    return pl.pallas_call(
        body,
        in_specs=in_specs,
        out_specs=[pl.BlockSpec(memory_space=pltpu.VMEM) for _ in outs],
        out_shape=[place(s, d) for s, d in outs],
        scratch_shapes=list(scratch),
        compiler_params=pltpu.CompilerParams(vmem_limit_bytes=limit << 20),
    )(*args)


def join_rows(scr, own, other):
    half = own.shape[0]
    scr[:half, :] = own[...]
    scr[half:, :] = other[...]


def place_rows(scr, sc, own, group, first_bit, source, target):
    near, first, second = group
    half, q = own.shape[0], near.shape[0]
    scr[:half, target] = own[:, target]
    b1, b2 = sc[1], sc[2]

    def at(r1, r2):
        p1 = 1 - b1 if r1 else b1
        p2 = 1 - b2 if r2 else b2
        return pl.ds(pl.multiple_of(half + q * (2 * p2 + p1), 16), q)

    scr[at(0, 0), target] = near[:, source]
    scr[at(1, 0) if first_bit == 1 else at(0, 1), target] = first[:, source]
    scr[at(0, 1) if first_bit == 1 else at(1, 0), target] = second[:q, source]
    scr[at(1, 1), target] = second[q:, source]


def place_mix(wg, wu, sc, own_g, own_u, e1, e2):
    ff = wg.shape[1]
    place_rows(wg, sc, own_g, e1, 1, slice(0, ff), slice(0, ff))
    place_rows(wu, sc, own_u, e2, 2, slice(0, ff), slice(0, ff))


def place_down(wd, sc, own, e1, e2):
    ff = wd.shape[1]
    tail = slice(ff, ff + ff // 2)
    place_rows(wd, sc, own, e1, 1, tail, slice(0, ff // 2))
    place_rows(wd, sc, own, e2, 2, tail, slice(ff // 2, ff))


def sequence_t(sc, local, own_recv, diag_recv, other_recv):
    diag = sc[3] == 1
    own = jnp.where(diag, local[...], own_recv[...].astype(f32))
    other = jnp.where(diag, diag_recv[...].astype(f32), other_recv[...].astype(f32))
    return jnp.concatenate([own, other], axis=0).T


def proj_body(sc, x_local, x_own, x_diag, x_other, g, w_own, w_other, x, normed, raw_q, kv, w):
    join_rows(w, w_own, w_other)
    v = sequence_t(sc, x_local, x_own, x_diag, x_other)
    x[...] = v
    n = (v * rms_scale(v) * g[0:1, :]).astype(bf16)
    normed[...] = n
    p = dot(n, w[...])
    qw = raw_q.shape[1]
    raw_q[...] = p[:, :qw]
    kv[...] = p[:, qw:]


def cot_body(sc, c_local, c_diag, c_off, cot):
    here = jnp.concatenate([c_local[...], c_diag[...].astype(f32)], axis=0)
    cot[...] = jnp.where(sc[3] == 1, here, c_off[...].astype(f32)).T


def cot_send_body(own, other, _, send):
    half = own.shape[0]
    send[:half, :] = own[...]
    send[half:, :] = other[...]


def attn_body(sc, raw_q, kv_mine, kv_theirs, mask, cos, sin, gq, gk, w_own, w_other, q, k, v,
              probs, heads, part, send, w):
    join_rows(w, w_own, w_other)
    first = sc[0] == 1
    c, s = cos[...], sin[...]
    hd = k.shape[1]
    raw_k = jnp.where(first, kv_mine[...], kv_theirs[...])
    raw_v = jnp.where(first, kv_theirs[...], kv_mine[...])
    key = rotate(raw_k * rms_scale(raw_k) * gk[...], c, s).astype(bf16)
    value = raw_v.astype(bf16)
    k[...] = key
    v[...] = value
    allowed = mask[...] > 0.0
    for h in range(q.shape[1] // hd):
        raw = raw_q[:, h * hd : (h + 1) * hd]
        query = rotate(raw * rms_scale(raw) * gq[...], c, s).astype(bf16)
        q[:, h * hd : (h + 1) * hd] = query
        logits = dot(query, key, ((1,), (1,))) * (hd**-0.5)
        weights = jnp.where(allowed, jnp.exp(logits), 0.0)
        p = weights / jnp.sum(weights, axis=1, keepdims=True)
        probs[h] = p
        heads[:, h * hd : (h + 1) * hd] = dot(p.astype(bf16), value).astype(bf16)
    out = dot(heads[...], w[...], ((1,), (1,)))
    part[...] = out
    send[...] = out.astype(bf16)


def mix_body(sc, x, own, recv, g, *refs):
    proj, mid, ffn_in, gate, up, hidden, wg, wu = refs[8:]
    place_mix(wg, wu, sc, refs[0], refs[1], refs[2:5], refs[5:8])
    y = own[...] + recv[...].astype(f32)
    proj[...] = y
    m = x[...] + y * rms_scale(y) * g[1:2, :]
    mid[...] = m
    n = (m * rms_scale(m) * g[2:3, :]).astype(bf16)
    ffn_in[...] = n
    ga = dot(n, wg[...])
    gate[...] = ga
    u = dot(n, wu[...])
    up[...] = u
    hidden[...] = (gelu_parts(ga)[1] * u).astype(bf16)


def down_body(sc, hidden, *refs):
    part, send, wd = refs[7:]
    place_down(wd, sc, refs[0], refs[1:4], refs[4:7])
    out = dot(hidden[...], wd[...], ((1,), (1,)))
    part[...] = out
    send[...] = out.astype(bf16)


def split_axis(sc, src, blocks, rows, left, d, emit):
    if d == "y":
        emit(0, 0, src(0, 0, rows), src(1, 0, rows))
        return
    groups = 1 << left.index(d)
    size = rows // groups
    half = size // 2
    b = sc[{1: 1, 2: 2, 4: 4}[d]]
    for block in range(blocks):
        for i in range(groups):
            mine = pl.multiple_of(i * size + b * half, 8)
            theirs = pl.multiple_of(i * size + (1 - b) * half, 8)
            emit(block, i * half, src(block, mine, half), src(block, theirs, half))


def split_grad(sc, left_t, right, send, keep, acc, d, col=0):
    split_sum(sc, dot(left_t, right), send, keep, acc, d, col)


def split_sum(sc, g, send, keep, acc, d, col=0):
    n = g.shape[1]
    cols = slice(col, col + n)
    half = g.shape[0] // 2
    if d == "y":
        send[0, :, cols] = g[half:].astype(bf16)
        keep[0, :, cols] = g[:half]
        return
    acc[0, :, cols] = g[:half]
    acc[1, :, cols] = g[half:]

    def emit(block, at, mine, theirs):
        rows = slice(at, at + mine.shape[0])
        send[block, rows, cols] = theirs.astype(bf16)
        keep[block, rows, cols] = mine

    split_axis(
        sc, lambda block, start, size: acc[block, pl.ds(start, size), cols], 2, half, TOP_BITS,
        d, emit,
    )


def stage_shapes(blocks, rows, n, d):
    if d == "y":
        return (1, rows, n)
    return (blocks, rows // 2, n)


def stage_body(d, left):
    def body(sc, keep_in, recv, send, keep, acc):
        blocks, rows, _ = keep_in.shape
        for block in range(blocks):
            acc[block] = keep_in[block] + recv[block].astype(f32)

        def emit(block, at, mine, theirs):
            span = slice(at, at + mine.shape[0])
            send[block, span, :] = theirs.astype(bf16)
            keep[block, span, :] = mine

        split_axis(
            sc, lambda block, start, size: acc[block, pl.ds(start, size), :], blocks, rows, left,
            d, emit,
        )

    return body


def last_sum_body(keep_in, recv, send):
    send[...] = (keep_in[...].astype(f32) + recv[...].astype(f32)).astype(bf16)


def assemble_body(order, widths):
    def body(sc, near, far, *outs):
        rows = near.shape[1]
        for part, ref in ((0, near), (1, far)):
            for j in range(2):
                rel = {order[0]: j, order[1]: part}
                p1 = 1 - sc[1] if rel[1] else sc[1]
                p2 = 1 - sc[2] if rel[2] else sc[2]
                at = pl.ds(pl.multiple_of((2 * p1 + p2) * rows, 8), rows)
                val = ref[j].astype(f32)
                col = 0
                for out, w in zip(outs, widths):
                    out[at, :] = val[:, col : col + w].astype(out.dtype)
                    col += w

    return body


def down_grad_body(sc, mid, own, recv, cot, g, hidden, out, out_send, grad_ffn, gain_part, send,
                   keep, acc):
    f = own[...] + recv[...].astype(f32)
    s = rms_scale(f)
    full = (mid[...] + f * s * g[3:4, :]).T
    half = full.shape[0] // 2
    out[...] = full[:half]
    out_send[...] = full[half:].astype(bf16)
    through, part = norm_back(cot[...], f, s, g[3:4, :])
    gain_part[...] = part
    gf = through.astype(bf16)
    grad_ffn[...] = gf
    split_grad(sc, gf.T, hidden[...], send, keep, acc, PLAN["down"][0])


def mix_grad_body(sc, grad_ffn, gate, up, ffn_in, *refs):
    s_gate, k_gate, s_up, k_up, part, send, wg, wu, wd, acc = refs[9:]
    place_down(wd, sc, refs[2], refs[3:6], refs[6:9])
    place_mix(wg, wu, sc, refs[0], refs[1], refs[3:6], refs[6:9])
    gh = dot(grad_ffn[...], wd[...])
    v = gate[...]
    t, gelu = gelu_parts(v)
    slope = 0.5 * (1.0 + t) + 0.5 * v * (1.0 - t * t) * (gelu_c * (1.0 + 3.0 * gelu_a * v * v))
    gg = (gh * up[...] * slope).astype(bf16)
    gu = (gh * gelu).astype(bf16)
    n_t = ffn_in[...].T
    split_grad(sc, n_t, gg, s_gate, k_gate, acc, PLAN["gate"][0])
    split_grad(sc, n_t, gu, s_up, k_up, acc, PLAN["up"][0])
    out = dot(gg, wg[...], ((1,), (1,))) + dot(gu, wu[...], ((1,), (1,)))
    part[...] = out
    send[...] = out.astype(bf16)


def attn_grad_body(sc, own, recv, mid, proj, cot, g, w_own, w_other, q, k, v, probs, raw_q, cos,
                   sin, gq, heads, grad_mid, pre_part, attn_part, kv_own, kv_send, grad_q,
                   q_part, out_send, out_keep, w, acc):
    join_rows(w, w_own, w_other)
    up = own[...] + recv[...].astype(f32)
    m = mid[...]
    through, part = norm_back(up, m, rms_scale(m), g[2:3, :])
    pre_part[...] = part
    gm = cot[...] + through
    grad_mid[...] = gm
    y = proj[...]
    through, part = norm_back(gm, y, rms_scale(y), g[1:2, :])
    attn_part[...] = part
    ga = through.astype(bf16)
    split_grad(sc, ga.T, heads[...], out_send, out_keep, acc, PLAN["out"][0])
    grad_heads = dot(ga, w[...]).astype(bf16)
    hd = k.shape[1]
    c, s = cos[...], sin[...]
    key, value = k[...], v[...]
    value_part, key_part, gain_part = 0.0, 0.0, 0.0
    scale = hd**-0.5
    for h in range(q.shape[1] // hd):
        cols = slice(h * hd, (h + 1) * hd)
        gh = grad_heads[:, cols]
        p = probs[h]
        value_part = value_part + dot(p.astype(bf16).T, gh)
        gp = dot(gh, value, ((1,), (1,)))
        delta = jnp.sum(p * gp, axis=1, keepdims=True)
        gs = (p * (gp - delta)).astype(bf16)
        gq_rot = dot(gs, key) * scale
        key_part = key_part + dot(gs.T, q[:, cols]) * scale
        raw = raw_q[:, cols]
        through, part = norm_back(rotate_back(gq_rot, c, s), raw, rms_scale(raw), gq[...])
        grad_q[:, cols] = through.astype(bf16)
        gain_part = gain_part + part
    q_part[...] = gain_part
    first = sc[0] == 1
    kv_own[...] = jnp.where(first, key_part, value_part)
    kv_send[...] = jnp.where(first, value_part, key_part)


def joint_body(sc, kv_own, kv_recv, kv_raw, cos, sin, gk, grad_q, normed, x,
               attn_part, pre_part, post_part, q_part, w_own, w_other, send, keep, part,
               part_send, w, acc):
    join_rows(w, w_own, w_other)
    total = kv_own[...] + kv_recv[...]
    raw = kv_raw[...]
    through, gain_part = norm_back(
        rotate_back(total, cos[...], sin[...]), raw, rms_scale(raw), gk[...]
    )
    first = sc[0] == 1
    k_part = jnp.where(first, gain_part, 0.0)
    kvg = jnp.where(first, through, total).astype(bf16)
    gq = grad_q[...]
    qw, kw = gq.shape[1], kvg.shape[1]
    n_t = normed[...].T
    d = PLAN["qkv"][0]
    split_grad(sc, n_t, gq, send, keep, acc, d, 0)
    split_grad(sc, n_t, kvg, send, keep, acc, d, qw)
    out = dot(gq, w[:, :qw], ((1,), (1,))) + dot(kvg, w[:, qw:], ((1,), (1,)))
    part[...] = out
    part_send[...] = out.astype(bf16)
    v = x[...]
    in_part = jnp.sum(out * v * rms_scale(v), axis=0, keepdims=True)
    diag = sc[3] == 1
    shared = [jnp.where(diag, ref[...], 0.0) for ref in (attn_part, pre_part, post_part)]
    half = v.shape[1] // 2
    wide = jnp.concatenate(
        [in_part] + shared + [jnp.zeros((gain_cols - 4, v.shape[1]), f32)], axis=0
    ).T
    ends = jnp.concatenate(
        [jnp.zeros((4, kw), f32), q_part[...], k_part, jnp.zeros((gain_cols - 6, kw), f32)],
        axis=0,
    ).T
    ends = jnp.concatenate([ends, jnp.zeros((half - kw, gain_cols), f32)], axis=0)
    gains = wide + jnp.concatenate([ends, ends], axis=0)
    split_sum(sc, gains, send, keep, acc, d, qw + kw)


def finish_body(sc, own, recv, key, value, gains):
    first = sc[0] == 1
    kw = key.shape[1]
    a, b = own[:, :kw].astype(f32), recv[:, :kw].astype(f32)
    key[...] = jnp.where(first, a, b)
    value[...] = jnp.where(first, b, a)
    gains[...] = (own[:, kw:].astype(f32) + recv[:, kw:].astype(f32)).T[: gains.shape[0]]


def input_body(own, recv, x, grad_mid, g, out, out_send):
    up = own[...] + recv[...].astype(f32)
    v = x[...]
    through, _ = norm_back(up, v, rms_scale(v), g[0:1, :])
    full = (grad_mid[...] + through).T
    half = full.shape[0] // 2
    out[...] = full[:half]
    out_send[...] = full[half:].astype(bf16)


def make_step(mesh):
    n_dp, n_row, n_col = mesh.shape["dp"], mesh.shape["row"], mesh.shape["col"]
    assert n_row == 2 and n_col == 2 and n_dp >= 8
    bits = []
    while (1 << len(bits)) < n_dp:
        bits.append(1 << len(bits))
    assert (1 << len(bits)) == n_dp
    extra = tuple(b for b in bits if b > 4)

    def swap_row(v):
        return lax.ppermute(v, "row", [(0, 1), (1, 0)])

    def swap_col(v):
        return lax.ppermute(v, "col", [(0, 1), (1, 0)])

    def swap_dp(v, bit):
        return lax.ppermute(v, "dp", [(i, i ^ bit) for i in range(n_dp)])

    def step(
        block_input, segment_ids, w_query, w_key, w_value, w_out, w_gate, w_up, w_down,
        gain_input, gain_attn, gain_ffn_pre, gain_ffn_post, gain_query, gain_key, out_cotangent,
    ):
        rows, half_width = block_input.shape
        width = 2 * half_width
        hd = w_key.shape[1]
        qw = w_query.shape[1]
        n_head = qw // hd
        ff = w_gate.shape[1]
        row = lax.axis_index("row")
        col = lax.axis_index("col")
        dp = lax.axis_index("dp")
        diag = row == col
        first_col = col == 0

        def bit_of(bit):
            return (dp // bit) % 2

        code = (1 - col) + 2 * bit_of(1) + 4 * bit_of(2) + 8 * (row == col) + 16 * bit_of(4)
        sc = (code >> jnp.arange(8, dtype=jnp.int32)) & 1

        def off_to_diag(v):
            return lax.ppermute(v, ("row", "col"), [(1, 3), (2, 0)])

        def diag_to_off_col(v):
            return lax.ppermute(v, ("row", "col"), [(0, 1), (3, 2)])

        def diag_to_off_row(v):
            return lax.ppermute(v, ("row", "col"), [(0, 2), (3, 1)])

        def chip_sequence(local, kind):
            local_t = local.T
            narrow = local_t.astype(kind)
            from_row = off_to_diag(narrow)
            return local_t, diag_to_off_col(narrow), from_row, diag_to_off_col(from_row)

        def other_rows(own, first_bit, second_bit):
            q = half_width // 4
            at = (2 * bit_of(2) + bit_of(1)) * q
            part = jnp.concatenate([lax.dynamic_slice_in_dim(w, at, q, 0) for w in own], axis=1)
            near = swap_row(part)
            first = swap_dp(near, first_bit)
            second = swap_dp(jnp.concatenate([near, first], axis=0), second_bit)
            return near, first, second

        x_pieces = chip_sequence(block_input, f32)
        joint_own = jnp.concatenate([w_query, jnp.where(first_col, w_key, w_value)], axis=1)
        w_joint = (joint_own, swap_row(joint_own))
        which = lax.broadcasted_iota(jnp.int32, (4, half_width), 0)
        gains_own = jnp.where(
            which == 0, gain_input,
            jnp.where(which == 1, gain_attn, jnp.where(which == 2, gain_ffn_pre, gain_ffn_post)),
        )
        gains = jnp.concatenate([gains_own, swap_row(gains_own)], axis=1)
        out_own = w_out.T
        wo = (out_own, swap_row(out_own))
        down_own = w_down.T
        e1 = other_rows((w_gate, down_own[:, : ff // 2]), 1, 2)
        e2 = other_rows((w_up, down_own[:, ff // 2 :]), 2, 1)
        cot_t = out_cotangent.T
        cot_narrow = cot_t.astype(bf16)
        cot_diag = off_to_diag(cot_narrow)

        segments = segment_ids[0]
        places = jnp.arange(rows, dtype=jnp.int32)
        allowed = (segments[:, None] == segments[None, :]) & (places[:, None] >= places[None, :])
        mask = allowed.astype(f32)
        offsets = jnp.sum(mask, axis=1) - 1.0
        frequency = rope_base ** (-(jnp.arange(hd // 2, dtype=f32) * 2.0 / hd))
        angles = offsets[:, None] * frequency
        cos, sin = jnp.cos(angles), jnp.sin(angles)
        gq, gk = gain_query[None], gain_key[None]

        t = rows
        joint_width = qw + hd
        wide_f, wide_b = ((t, width), f32), ((t, width), bf16)
        ffn_scratch = [pltpu.VMEM((width, ff), bf16) for _ in range(3)]
        x, normed, raw_q, kv_mine = call(
            proj_body, [wide_f, wide_b, ((t, qw), f32), ((t, hd), f32)],
            *x_pieces, gains, *w_joint, scalars=sc,
            scratch=[pltpu.VMEM((width, joint_width), bf16)],
        )
        kv_theirs = swap_col(kv_mine)
        q, k, v, probs, heads, part, send = call(
            attn_body,
            [((t, qw), bf16), ((t, hd), bf16), ((t, hd), bf16), ((n_head, t, t), f32),
             ((t, qw), bf16), wide_f, wide_b],
            raw_q, kv_mine, kv_theirs, mask, cos, sin, gq, gk, *wo, scalars=sc,
            scratch=[pltpu.VMEM((width, qw), bf16)],
        )
        proj, mid, ffn_in, gate, up, hidden = call(
            mix_body,
            [wide_f, wide_f, wide_b, ((t, ff), f32), ((t, ff), f32), ((t, ff), bf16)],
            x, part, swap_col(send), gains, w_gate, w_up, *e1, *e2, scalars=sc,
            scratch=ffn_scratch[:2],
        )
        (cot_send,) = call(cot_send_body, [((width, t), bf16)], cot_narrow, cot_diag, mid)
        cot_off = diag_to_off_col(cot_send)
        (cotangent,) = call(cot_body, [wide_f], cot_t, cot_diag, cot_off, scalars=sc)
        part, send = call(
            down_body, [wide_f, wide_b], hidden, down_own, *e1, *e2, scalars=sc,
            scratch=ffn_scratch[:1],
        )

        def first_shapes(name, n):
            s = stage_shapes(2, half_width, n, PLAN[name][0])
            return [(s, bf16), (s, f32)]

        def swap(v, d):
            return swap_row(v) if d == "y" else swap_dp(v, d)

        def more_bits(cur):
            n = cur.shape[-1]
            for bit in extra:
                size = cur.shape[1] // 2
                halves = cur.reshape(2, size, n).astype(f32)
                b = bit_of(bit)
                sent = lax.dynamic_index_in_dim(halves, 1 - b, 0).astype(bf16)
                got = swap_dp(sent, bit).astype(f32)
                cur = lax.dynamic_index_in_dim(halves, b, 0) + got
            cur = cur.astype(bf16)
            for bit in reversed(extra):
                theirs = swap_dp(cur, bit)
                b = bit_of(bit)
                cur = jnp.concatenate(
                    [jnp.where(b == 0, cur, theirs), jnp.where(b == 0, theirs, cur)], axis=1
                )
            return cur

        def grad_sum(name, send, keep, outs):
            n = keep.shape[-1]
            order = PLAN[name]
            left = list(TOP_BITS)
            if order[0] != "y":
                left.remove(order[0])
            for stage, d in enumerate(order[:-1]):
                recv = swap(send, d)
                if stage == len(order) - 2:
                    break
                nxt = order[stage + 1]
                blocks, r, _ = keep.shape
                shape = stage_shapes(blocks, r, n, nxt)
                send, keep = call(
                    stage_body(nxt, tuple(left)),
                    [(shape, bf16), (shape, f32)], keep, recv, scalars=sc,
                    scratch=[pltpu.VMEM((blocks, r, n), f32)],
                )
                if nxt != "y":
                    left.remove(nxt)
            (cur,) = call(last_sum_body, [(keep.shape, bf16)], keep, recv)
            stage = len(order) - 1
            recv = swap_dp(cur, order[-1])
            (cur,) = call(last_sum_body, [(cur.shape, bf16)], cur, recv)
            if extra:
                cur = more_bits(cur)
            for d in GATHER[name]:
                stage += 1
                theirs = swap_dp(cur, d)
                if d != GATHER[name][-1]:
                    cur = jnp.concatenate([cur, theirs], axis=0)
            return call(
                assemble_body(GATHER[name], [w for w, _ in outs]),
                [((half_width, w), dt) for w, dt in outs], cur, theirs, scalars=sc, out_hbm=True,
            )

        out_pair = [((half_width, t), f32), ((half_width, t), bf16)]
        out_own_t, out_send, grad_ffn, post_part, s_down, k_down = call(
            down_grad_body,
            out_pair + [wide_b, ((1, width), f32)] + first_shapes("down", ff),
            mid, part, swap_col(send), cotangent, gains, hidden, scalars=sc,
            scratch=[pltpu.VMEM((2, half_width, ff), f32)],
        )
        (down_sum,) = grad_sum("down", s_down, k_down, [(ff, f32)])
        s_gate, k_gate, s_up, k_up, part, send = call(
            mix_grad_body,
            first_shapes("gate", ff) + first_shapes("up", ff) + [wide_f, wide_b],
            grad_ffn, gate, up, ffn_in, w_gate, w_up, down_own, *e1, *e2, scalars=sc,
            scratch=ffn_scratch + [pltpu.VMEM((2, half_width, ff), f32)],
        )
        (gate_sum,) = grad_sum("gate", s_gate, k_gate, [(ff, f32)])
        (up_sum,) = grad_sum("up", s_up, k_up, [(ff, f32)])
        grad_mid, pre_part, attn_part, kv_own, kv_send, grad_q, q_part, s_out, k_out = call(
            attn_grad_body,
            [wide_f, ((1, width), f32), ((1, width), f32), ((t, hd), f32), ((t, hd), f32),
             ((t, qw), bf16), ((1, hd), f32)] + first_shapes("out", qw),
            part, swap_col(send), mid, proj, cotangent, gains, *wo, q, k, v, probs,
            raw_q, cos, sin, gq, heads, scalars=sc,
            scratch=[pltpu.VMEM((width, qw), bf16), pltpu.VMEM((2, half_width, qw), f32)],
        )
        (out_sum,) = grad_sum("out", s_out, k_out, [(qw, f32)])
        n_qkv = joint_width + gain_cols
        s_qkv, k_qkv, part, send = call(
            joint_body, first_shapes("qkv", n_qkv) + [wide_f, wide_b],
            kv_own, swap_col(kv_send), kv_mine, cos, sin, gk, grad_q, normed,
            x, attn_part, pre_part, post_part, q_part, *w_joint, scalars=sc,
            scratch=[pltpu.VMEM((width, joint_width), bf16),
                     pltpu.VMEM((2, half_width, n_qkv), f32)],
        )
        query_sum, kv_sum = grad_sum(
            "qkv", s_qkv, k_qkv, [(qw, f32), (hd + gain_cols, bf16)]
        )
        in_own_t, in_send = call(
            input_body, out_pair,
            part, swap_col(send), x, grad_mid, gains,
        )
        both = diag_to_off_row(jnp.concatenate([out_send, in_send], axis=0)).astype(f32)
        block_output = jnp.where(diag, out_own_t, both[:half_width]).T
        input_grad = jnp.where(diag, in_own_t, both[half_width:]).T
        key_sum, value_sum, gain_sum = call(
            finish_body,
            [((half_width, hd), f32), ((half_width, hd), f32), ((8, half_width), f32)],
            kv_sum, swap_col(kv_sum), scalars=sc, out_hbm=True,
        )
        return (
            block_output, input_grad, query_sum, key_sum, value_sum, out_sum.T,
            gate_sum, up_sum, down_sum.T,
            gain_sum[0], gain_sum[1], gain_sum[2], gain_sum[3],
            gain_sum[4, :hd], gain_sum[5, :hd],
        )

    return step


def solution(mesh):
    rows_by_width = P(("dp", "col"), "row")
    in_specs = (
        rows_by_width, P(("dp", "row"), None), P("row", "col"), P("row", None), P("row", None),
        P("col", "row"), P("row", "col"), P("row", "col"), P("col", "row"),
        P("row"), P("row"), P("row"), P("row"), P(), P(), rows_by_width,
    )
    out_specs = (
        rows_by_width, rows_by_width, P("row", "col"), P("row", None), P("row", None),
        P("col", "row"), P("row", "col"), P("row", "col"), P("col", "row"),
        P("row"), P("row"), P("row"), P("row"), P(), P(),
    )
    return jax.shard_map(
        make_step(mesh), mesh=mesh, in_specs=in_specs, out_specs=out_specs, check_vma=False
    )
```

```python
import jax
import jax.numpy as jnp
from jax import lax
from jax.experimental import pallas as pl
from jax.experimental.pallas import tpu as pltpu
from jax.sharding import PartitionSpec as P

eps_norm = 1e-06
rope_base = 1000000.0
bf16 = jnp.bfloat16
f32 = jnp.float32
gelu_c = (2.0 / 3.141592653589793) ** 0.5
gelu_a = 0.044715
gain_cols = 128


PLAN = {
    "down": ("y", 2, 1, 4),
    "gate": (2, 1, "y", 4),
    "up": (1, 2, "y", 4),
    "out": ("y", 2, 1, 4),
    "qkv": ("y", 2, 1, 4),
}
GATHER = {"down": (2, 1), "gate": (1, 2), "up": (2, 1), "out": (2, 1), "qkv": (1, 2)}
TOP_BITS = (1, 2, 4)


def dot(left, right, contract=((1,), (0,))):
    return lax.dot_general(left, right, (contract, ((), ())), preferred_element_type=f32)


def rms_scale(values):
    return lax.rsqrt(jnp.mean(values * values, axis=-1, keepdims=True) + eps_norm)


def norm_back(upstream, values, inv_rms, gain_vector):
    weighted = upstream * gain_vector
    width_sum = jnp.sum(weighted * values, axis=1, keepdims=True)
    through = inv_rms * weighted - values * (inv_rms**3 * width_sum / values.shape[1])
    return through, jnp.sum(upstream * values * inv_rms, axis=0, keepdims=True)


def rotate(values, cosine_table, sine_table):
    half = values.shape[1] // 2
    a, b = values[:, :half], values[:, half:]
    return jnp.concatenate(
        [a * cosine_table - b * sine_table, b * cosine_table + a * sine_table], axis=1
    )


def rotate_back(values, cosine_table, sine_table):
    return rotate(values, cosine_table, -sine_table)


def gelu_parts(v):
    t = jnp.tanh(gelu_c * (v + gelu_a * v * v * v))
    return t, 0.5 * v * (1.0 + t)


def call(body, outs, *args, scalars=None, scratch=(), out_hbm=False, limit=24):
    in_specs = [pl.BlockSpec(memory_space=pltpu.VMEM) for _ in args]
    args = tuple(pltpu.with_memory_space_constraint(v, pltpu.VMEM) for v in args)
    if scalars is not None:
        in_specs = [pl.BlockSpec(memory_space=pltpu.SMEM)] + in_specs
        args = (scalars,) + args
    in_hbm = len(outs) if out_hbm is True else int(out_hbm)
    place = [jax.ShapeDtypeStruct] * in_hbm + [pltpu.VMEM] * (len(outs) - in_hbm)
    return pl.pallas_call(
        body,
        in_specs=in_specs,
        out_specs=[pl.BlockSpec(memory_space=pltpu.VMEM) for _ in outs],
        out_shape=[at(s, d) for at, (s, d) in zip(place, outs)],
        scratch_shapes=list(scratch),
        compiler_params=pltpu.CompilerParams(vmem_limit_bytes=limit << 20),
    )(*args)


def join_rows(scr, own, other):
    half = own.shape[0]
    scr[:half, :] = own[...]
    scr[half:, :] = other[...]


def place_rows(scr, sc, own, group, first_bit, source, target):
    near, first, second = group
    half, q = own.shape[0], near.shape[0]
    scr[:half, target] = own[:, target]
    b1, b2 = sc[1], sc[2]

    def at(r1, r2):
        p1 = 1 - b1 if r1 else b1
        p2 = 1 - b2 if r2 else b2
        return pl.ds(pl.multiple_of(half + q * (2 * p2 + p1), 16), q)

    scr[at(0, 0), target] = near[:, source]
    scr[at(1, 0) if first_bit == 1 else at(0, 1), target] = first[:, source]
    scr[at(0, 1) if first_bit == 1 else at(1, 0), target] = second[:q, source]
    scr[at(1, 1), target] = second[q:, source]


def place_mix(wg, wu, sc, own_g, own_u, e1, e2):
    ff = wg.shape[1]
    place_rows(wg, sc, own_g, e1, 1, slice(0, ff), slice(0, ff))
    place_rows(wu, sc, own_u, e2, 2, slice(0, ff), slice(0, ff))


def place_down(wd, sc, own, e1, e2):
    ff = wd.shape[1]
    tail = slice(ff, ff + ff // 2)
    place_rows(wd, sc, own, e1, 1, tail, slice(0, ff // 2))
    place_rows(wd, sc, own, e2, 2, tail, slice(ff // 2, ff))


def sequence_t(sc, local, own_recv, diag_recv, other_recv):
    diag = sc[3] == 1
    own = jnp.where(diag, local[...], own_recv[...].astype(f32))
    other = jnp.where(diag, diag_recv[...].astype(f32), other_recv[...].astype(f32))
    return jnp.concatenate([own, other], axis=0).T


def proj_body(sc, x_local, x_own, x_diag, x_other, g, w_own, w_other, x, normed, raw_q, kv, w):
    join_rows(w, w_own, w_other)
    v = sequence_t(sc, x_local, x_own, x_diag, x_other)
    x[...] = v
    n = (v * rms_scale(v) * g[0:1, :]).astype(bf16)
    normed[...] = n
    p = dot(n, w[...])
    qw = raw_q.shape[1]
    raw_q[...] = p[:, :qw]
    kv[...] = p[:, qw:]


def cot_body(sc, c_local, c_diag, c_off, cot):
    here = jnp.concatenate([c_local[...], c_diag[...].astype(f32)], axis=0)
    cot[...] = jnp.where(sc[3] == 1, here, c_off[...].astype(f32)).T


def cot_send_body(own, other, _, send):
    half = own.shape[0]
    send[:half, :] = own[...]
    send[half:, :] = other[...]


def attn_body(sc, raw_q, kv_mine, kv_theirs, mask, cos, sin, gq, gk, w_own, w_other, q, k, v,
              probs, heads, part, send, w):
    join_rows(w, w_own, w_other)
    first = sc[0] == 1
    c, s = cos[...], sin[...]
    hd = k.shape[1]
    raw_k = jnp.where(first, kv_mine[...], kv_theirs[...])
    raw_v = jnp.where(first, kv_theirs[...], kv_mine[...])
    key = rotate(raw_k * rms_scale(raw_k) * gk[...], c, s).astype(bf16)
    value = raw_v.astype(bf16)
    k[...] = key
    v[...] = value
    allowed = mask[...] > 0.0
    for h in range(q.shape[1] // hd):
        raw = raw_q[:, h * hd : (h + 1) * hd]
        query = rotate(raw * rms_scale(raw) * gq[...], c, s).astype(bf16)
        q[:, h * hd : (h + 1) * hd] = query
        logits = dot(query, key, ((1,), (1,))) * (hd**-0.5)
        weights = jnp.where(allowed, jnp.exp(logits), 0.0)
        p = weights / jnp.sum(weights, axis=1, keepdims=True)
        probs[h] = p
        heads[:, h * hd : (h + 1) * hd] = dot(p.astype(bf16), value).astype(bf16)
    out = dot(heads[...], w[...], ((1,), (1,)))
    part[...] = out
    send[...] = out.astype(bf16)


def mix_body(sc, x, own, recv, g, *refs):
    proj, mid, ffn_in, gate, up, hidden, wg, wu = refs[8:]
    place_mix(wg, wu, sc, refs[0], refs[1], refs[2:5], refs[5:8])
    y = own[...] + recv[...].astype(f32)
    proj[...] = y
    m = x[...] + y * rms_scale(y) * g[1:2, :]
    mid[...] = m
    n = (m * rms_scale(m) * g[2:3, :]).astype(bf16)
    ffn_in[...] = n
    ga = dot(n, wg[...])
    gate[...] = ga
    u = dot(n, wu[...])
    up[...] = u
    hidden[...] = (gelu_parts(ga)[1] * u).astype(bf16)


def down_body(sc, hidden, *refs):
    part, send, wd = refs[7:]
    place_down(wd, sc, refs[0], refs[1:4], refs[4:7])
    out = dot(hidden[...], wd[...], ((1,), (1,)))
    part[...] = out
    send[...] = out.astype(bf16)


def split_axis(sc, src, blocks, rows, left, d, emit):
    if d == "y":
        emit(0, 0, src(0, 0, rows), src(1, 0, rows))
        return
    groups = 1 << left.index(d)
    size = rows // groups
    half = size // 2
    b = sc[{1: 1, 2: 2, 4: 4}[d]]
    for block in range(blocks):
        for i in range(groups):
            mine = pl.multiple_of(i * size + b * half, 8)
            theirs = pl.multiple_of(i * size + (1 - b) * half, 8)
            emit(block, i * half, src(block, mine, half), src(block, theirs, half))


def split_grad(sc, left_t, right, send, keep, acc, d, col=0):
    split_sum(sc, dot(left_t, right), send, keep, acc, d, col)


def split_sum(sc, g, send, keep, acc, d, col=0):
    n = g.shape[1]
    cols = slice(col, col + n)
    half = g.shape[0] // 2
    if d == "y":
        send[0, :, cols] = g[half:].astype(bf16)
        keep[0, :, cols] = g[:half]
        return
    acc[0, :, cols] = g[:half]
    acc[1, :, cols] = g[half:]

    def emit(block, at, mine, theirs):
        rows = slice(at, at + mine.shape[0])
        send[block, rows, cols] = theirs.astype(bf16)
        keep[block, rows, cols] = mine

    split_axis(
        sc, lambda block, start, size: acc[block, pl.ds(start, size), cols], 2, half, TOP_BITS,
        d, emit,
    )


def stage_shapes(blocks, rows, n, d):
    if d == "y":
        return (1, rows, n)
    return (blocks, rows // 2, n)


def stage_body(d, left):
    def body(sc, keep_in, recv, send, keep, acc):
        blocks, rows, _ = keep_in.shape
        for block in range(blocks):
            acc[block] = keep_in[block] + recv[block].astype(f32)

        def emit(block, at, mine, theirs):
            span = slice(at, at + mine.shape[0])
            send[block, span, :] = theirs.astype(bf16)
            keep[block, span, :] = mine

        split_axis(
            sc, lambda block, start, size: acc[block, pl.ds(start, size), :], blocks, rows, left,
            d, emit,
        )

    return body


def last_sum_body(keep_in, recv, send):
    send[...] = (keep_in[...].astype(f32) + recv[...].astype(f32)).astype(bf16)


def assemble_body(order, widths):
    def body(sc, near, far, *outs):
        rows = near.shape[1]
        for part, ref in ((0, near), (1, far)):
            for j in range(2):
                rel = {order[0]: j, order[1]: part}
                p1 = 1 - sc[1] if rel[1] else sc[1]
                p2 = 1 - sc[2] if rel[2] else sc[2]
                at = pl.ds(pl.multiple_of((2 * p1 + p2) * rows, 8), rows)
                val = ref[j].astype(f32)
                col = 0
                for out, w in zip(outs, widths):
                    out[at, :] = val[:, col : col + w].astype(out.dtype)
                    col += w

    return body


def down_grad_body(sc, mid, own, recv, cot, g, hidden, out, out_send, grad_ffn, gain_part, send,
                   keep, acc):
    f = own[...] + recv[...].astype(f32)
    s = rms_scale(f)
    full = (mid[...] + f * s * g[3:4, :]).T
    half = full.shape[0] // 2
    out[...] = full[:half]
    out_send[...] = full[half:].astype(bf16)
    through, part = norm_back(cot[...], f, s, g[3:4, :])
    gain_part[...] = part
    gf = through.astype(bf16)
    grad_ffn[...] = gf
    split_grad(sc, gf.T, hidden[...], send, keep, acc, PLAN["down"][0])


def mix_grad_body(sc, grad_ffn, gate, up, ffn_in, *refs):
    s_gate, k_gate, s_up, k_up, part, send, wg, wu, wd, acc = refs[9:]
    place_down(wd, sc, refs[2], refs[3:6], refs[6:9])
    place_mix(wg, wu, sc, refs[0], refs[1], refs[3:6], refs[6:9])
    gh = dot(grad_ffn[...], wd[...])
    v = gate[...]
    t, gelu = gelu_parts(v)
    slope = 0.5 * (1.0 + t) + 0.5 * v * (1.0 - t * t) * (gelu_c * (1.0 + 3.0 * gelu_a * v * v))
    gg = (gh * up[...] * slope).astype(bf16)
    gu = (gh * gelu).astype(bf16)
    n_t = ffn_in[...].T
    split_grad(sc, n_t, gg, s_gate, k_gate, acc, PLAN["gate"][0])
    split_grad(sc, n_t, gu, s_up, k_up, acc, PLAN["up"][0])
    out = dot(gg, wg[...], ((1,), (1,))) + dot(gu, wu[...], ((1,), (1,)))
    part[...] = out
    send[...] = out.astype(bf16)


def attn_grad_body(sc, own, recv, mid, proj, cot, g, w_own, w_other, q, k, v, probs, raw_q, cos,
                   sin, gq, heads, grad_mid, pre_part, attn_part, kv_own, kv_send, grad_q,
                   q_part, out_send, out_keep, w, acc):
    join_rows(w, w_own, w_other)
    up = own[...] + recv[...].astype(f32)
    m = mid[...]
    through, part = norm_back(up, m, rms_scale(m), g[2:3, :])
    pre_part[...] = part
    gm = cot[...] + through
    grad_mid[...] = gm
    y = proj[...]
    through, part = norm_back(gm, y, rms_scale(y), g[1:2, :])
    attn_part[...] = part
    ga = through.astype(bf16)
    split_grad(sc, ga.T, heads[...], out_send, out_keep, acc, PLAN["out"][0])
    grad_heads = dot(ga, w[...]).astype(bf16)
    hd = k.shape[1]
    c, s = cos[...], sin[...]
    key, value = k[...], v[...]
    value_part, key_part, gain_part = 0.0, 0.0, 0.0
    scale = hd**-0.5
    for h in range(q.shape[1] // hd):
        cols = slice(h * hd, (h + 1) * hd)
        gh = grad_heads[:, cols]
        p = probs[h]
        value_part = value_part + dot(p.astype(bf16).T, gh)
        gp = dot(gh, value, ((1,), (1,)))
        delta = jnp.sum(p * gp, axis=1, keepdims=True)
        gs = (p * (gp - delta)).astype(bf16)
        gq_rot = dot(gs, key) * scale
        key_part = key_part + dot(gs.T, q[:, cols]) * scale
        raw = raw_q[:, cols]
        through, part = norm_back(rotate_back(gq_rot, c, s), raw, rms_scale(raw), gq[...])
        grad_q[:, cols] = through.astype(bf16)
        gain_part = gain_part + part
    q_part[...] = gain_part
    first = sc[0] == 1
    kv_own[...] = jnp.where(first, key_part, value_part)
    kv_send[...] = jnp.where(first, value_part, key_part)


def joint_body(sc, kv_own, kv_recv, kv_raw, cos, sin, gk, grad_q, normed, x,
               attn_part, pre_part, post_part, q_part, w_own, w_other, send, keep, part,
               part_send, w, acc):
    join_rows(w, w_own, w_other)
    total = kv_own[...] + kv_recv[...]
    raw = kv_raw[...]
    through, gain_part = norm_back(
        rotate_back(total, cos[...], sin[...]), raw, rms_scale(raw), gk[...]
    )
    first = sc[0] == 1
    k_part = jnp.where(first, gain_part, 0.0)
    kvg = jnp.where(first, through, total).astype(bf16)
    gq = grad_q[...]
    qw, kw = gq.shape[1], kvg.shape[1]
    n_t = normed[...].T
    d = PLAN["qkv"][0]
    split_grad(sc, n_t, gq, send, keep, acc, d, 0)
    split_grad(sc, n_t, kvg, send, keep, acc, d, qw)
    out = dot(gq, w[:, :qw], ((1,), (1,))) + dot(kvg, w[:, qw:], ((1,), (1,)))
    part[...] = out
    part_send[...] = out.astype(bf16)
    v = x[...]
    in_part = jnp.sum(out * v * rms_scale(v), axis=0, keepdims=True)
    diag = sc[3] == 1
    shared = [jnp.where(diag, ref[...], 0.0) for ref in (attn_part, pre_part, post_part)]
    half = v.shape[1] // 2
    wide = jnp.concatenate(
        [in_part] + shared + [jnp.zeros((gain_cols - 4, v.shape[1]), f32)], axis=0
    ).T
    ends = jnp.concatenate(
        [jnp.zeros((4, kw), f32), q_part[...], k_part, jnp.zeros((gain_cols - 6, kw), f32)],
        axis=0,
    ).T
    ends = jnp.concatenate([ends, jnp.zeros((half - kw, gain_cols), f32)], axis=0)
    gains = wide + jnp.concatenate([ends, ends], axis=0)
    split_sum(sc, gains, send, keep, acc, d, qw + kw)


def finish_body(sc, own, recv, key, value, gains):
    first = sc[0] == 1
    kw = key.shape[1]
    a, b = own[:, :kw].astype(f32), recv[:, :kw].astype(f32)
    key[...] = jnp.where(first, a, b)
    value[...] = jnp.where(first, b, a)
    gains[...] = (own[:, kw:].astype(f32) + recv[:, kw:].astype(f32)).T[: gains.shape[0]]


def input_body(own, recv, x, grad_mid, g, out, out_send):
    up = own[...] + recv[...].astype(f32)
    v = x[...]
    through, _ = norm_back(up, v, rms_scale(v), g[0:1, :])
    full = (grad_mid[...] + through).T
    half = full.shape[0] // 2
    out[...] = full[:half]
    out_send[...] = full[half:].astype(bf16)


def make_step(mesh):
    n_dp, n_row, n_col = mesh.shape["dp"], mesh.shape["row"], mesh.shape["col"]
    assert n_row == 2 and n_col == 2 and n_dp >= 8
    bits = []
    while (1 << len(bits)) < n_dp:
        bits.append(1 << len(bits))
    assert (1 << len(bits)) == n_dp
    extra = tuple(b for b in bits if b > 4)

    def swap_row(v):
        return lax.ppermute(v, "row", [(0, 1), (1, 0)])

    def swap_col(v):
        return lax.ppermute(v, "col", [(0, 1), (1, 0)])

    def swap_dp(v, bit):
        return lax.ppermute(v, "dp", [(i, i ^ bit) for i in range(n_dp)])

    def step(
        block_input, segment_ids, w_query, w_key, w_value, w_out, w_gate, w_up, w_down,
        gain_input, gain_attn, gain_ffn_pre, gain_ffn_post, gain_query, gain_key, out_cotangent,
    ):
        rows, half_width = block_input.shape
        width = 2 * half_width
        hd = w_key.shape[1]
        qw = w_query.shape[1]
        n_head = qw // hd
        ff = w_gate.shape[1]
        row = lax.axis_index("row")
        col = lax.axis_index("col")
        dp = lax.axis_index("dp")
        diag = row == col
        first_col = col == 0

        def bit_of(bit):
            return (dp // bit) % 2

        code = (1 - col) + 2 * bit_of(1) + 4 * bit_of(2) + 8 * (row == col) + 16 * bit_of(4)
        sc = (code >> jnp.arange(8, dtype=jnp.int32)) & 1

        def off_to_diag(v):
            return lax.ppermute(v, ("row", "col"), [(1, 3), (2, 0)])

        def diag_to_off_col(v):
            return lax.ppermute(v, ("row", "col"), [(0, 1), (3, 2)])

        def diag_to_off_row(v):
            return lax.ppermute(v, ("row", "col"), [(0, 2), (3, 1)])

        def chip_sequence(local, kind):
            local_t = local.T
            narrow = local_t.astype(kind)
            from_row = off_to_diag(narrow)
            return local_t, diag_to_off_col(narrow), from_row, diag_to_off_col(from_row)

        def other_rows(own, first_bit, second_bit):
            q = half_width // 4
            at = (2 * bit_of(2) + bit_of(1)) * q
            part = jnp.concatenate([lax.dynamic_slice_in_dim(w, at, q, 0) for w in own], axis=1)
            near = swap_row(part)
            first = swap_dp(near, first_bit)
            second = swap_dp(jnp.concatenate([near, first], axis=0), second_bit)
            return near, first, second

        x_pieces = chip_sequence(block_input, f32)
        joint_own = jnp.concatenate([w_query, jnp.where(first_col, w_key, w_value)], axis=1)
        w_joint = (joint_own, swap_row(joint_own))
        which = lax.broadcasted_iota(jnp.int32, (4, half_width), 0)
        gains_own = jnp.where(
            which == 0, gain_input,
            jnp.where(which == 1, gain_attn, jnp.where(which == 2, gain_ffn_pre, gain_ffn_post)),
        )
        gains = jnp.concatenate([gains_own, swap_row(gains_own)], axis=1)
        out_own = w_out.T
        wo = (out_own, swap_row(out_own))
        down_own = w_down.T
        e1 = other_rows((w_gate, down_own[:, : ff // 2]), 1, 2)
        e2 = other_rows((w_up, down_own[:, ff // 2 :]), 2, 1)
        cot_t = out_cotangent.T
        cot_narrow = cot_t.astype(bf16)
        cot_diag = off_to_diag(cot_narrow)

        segments = segment_ids[0]
        places = jnp.arange(rows, dtype=jnp.int32)
        allowed = (segments[:, None] == segments[None, :]) & (places[:, None] >= places[None, :])
        mask = allowed.astype(f32)
        offsets = jnp.sum(mask, axis=1) - 1.0
        frequency = rope_base ** (-(jnp.arange(hd // 2, dtype=f32) * 2.0 / hd))
        angles = offsets[:, None] * frequency
        cos, sin = jnp.cos(angles), jnp.sin(angles)
        gq, gk = gain_query[None], gain_key[None]

        t = rows
        joint_width = qw + hd
        wide_f, wide_b = ((t, width), f32), ((t, width), bf16)
        ffn_scratch = [pltpu.VMEM((width, ff), bf16) for _ in range(3)]
        x, normed, raw_q, kv_mine = call(
            proj_body, [wide_f, wide_b, ((t, qw), f32), ((t, hd), f32)],
            *x_pieces, gains, *w_joint, scalars=sc,
            scratch=[pltpu.VMEM((width, joint_width), bf16)],
        )
        kv_theirs = swap_col(kv_mine)
        q, k, v, probs, heads, part, send = call(
            attn_body,
            [((t, qw), bf16), ((t, hd), bf16), ((t, hd), bf16), ((n_head, t, t), f32),
             ((t, qw), bf16), wide_f, wide_b],
            raw_q, kv_mine, kv_theirs, mask, cos, sin, gq, gk, *wo, scalars=sc,
            scratch=[pltpu.VMEM((width, qw), bf16)],
        )
        proj, mid, ffn_in, gate, up, hidden = call(
            mix_body,
            [wide_f, wide_f, wide_b, ((t, ff), f32), ((t, ff), f32), ((t, ff), bf16)],
            x, part, swap_col(send), gains, w_gate, w_up, *e1, *e2, scalars=sc,
            scratch=ffn_scratch[:2],
        )
        (cot_send,) = call(cot_send_body, [((width, t), bf16)], cot_narrow, cot_diag, mid)
        cot_off = diag_to_off_col(cot_send)
        (cotangent,) = call(cot_body, [wide_f], cot_t, cot_diag, cot_off, scalars=sc)
        part, send = call(
            down_body, [wide_f, wide_b], hidden, down_own, *e1, *e2, scalars=sc,
            scratch=ffn_scratch[:1],
        )

        def first_shapes(name, n):
            s = stage_shapes(2, half_width, n, PLAN[name][0])
            return [(s, bf16), (s, f32)]

        def swap(v, d):
            return swap_row(v) if d == "y" else swap_dp(v, d)

        def more_bits(cur):
            n = cur.shape[-1]
            for bit in extra:
                size = cur.shape[1] // 2
                halves = cur.reshape(2, size, n).astype(f32)
                b = bit_of(bit)
                sent = lax.dynamic_index_in_dim(halves, 1 - b, 0).astype(bf16)
                got = swap_dp(sent, bit).astype(f32)
                cur = lax.dynamic_index_in_dim(halves, b, 0) + got
            cur = cur.astype(bf16)
            for bit in reversed(extra):
                theirs = swap_dp(cur, bit)
                b = bit_of(bit)
                cur = jnp.concatenate(
                    [jnp.where(b == 0, cur, theirs), jnp.where(b == 0, theirs, cur)], axis=1
                )
            return cur

        def grad_sum(name, send, keep, outs):
            n = keep.shape[-1]
            order = PLAN[name]
            left = list(TOP_BITS)
            if order[0] != "y":
                left.remove(order[0])
            for stage, d in enumerate(order[:-1]):
                recv = swap(send, d)
                if stage == len(order) - 2:
                    break
                nxt = order[stage + 1]
                blocks, r, _ = keep.shape
                shape = stage_shapes(blocks, r, n, nxt)
                send, keep = call(
                    stage_body(nxt, tuple(left)),
                    [(shape, bf16), (shape, f32)], keep, recv, scalars=sc,
                    scratch=[pltpu.VMEM((blocks, r, n), f32)],
                )
                if nxt != "y":
                    left.remove(nxt)
            (cur,) = call(last_sum_body, [(keep.shape, bf16)], keep, recv)
            stage = len(order) - 1
            recv = swap_dp(cur, order[-1])
            (cur,) = call(last_sum_body, [(cur.shape, bf16)], cur, recv)
            if extra:
                cur = more_bits(cur)
            for d in GATHER[name]:
                stage += 1
                theirs = swap_dp(cur, d)
                if d != GATHER[name][-1]:
                    cur = jnp.concatenate([cur, theirs], axis=0)
            return call(
                assemble_body(GATHER[name], [w for w, _ in outs]),
                [((half_width, w), dt) for w, dt in outs], cur, theirs, scalars=sc, out_hbm=True,
            )

        out_pair = [((half_width, t), f32), ((half_width, t), bf16)]
        out_own_t, out_send, grad_ffn, post_part, s_down, k_down = call(
            down_grad_body,
            out_pair + [wide_b, ((1, width), f32)] + first_shapes("down", ff),
            mid, part, swap_col(send), cotangent, gains, hidden, scalars=sc,
            scratch=[pltpu.VMEM((2, half_width, ff), f32)],
        )
        (down_sum,) = grad_sum("down", s_down, k_down, [(ff, f32)])
        s_gate, k_gate, s_up, k_up, part, send = call(
            mix_grad_body,
            first_shapes("gate", ff) + first_shapes("up", ff) + [wide_f, wide_b],
            grad_ffn, gate, up, ffn_in, w_gate, w_up, down_own, *e1, *e2, scalars=sc,
            scratch=ffn_scratch + [pltpu.VMEM((2, half_width, ff), f32)],
        )
        (gate_sum,) = grad_sum("gate", s_gate, k_gate, [(ff, f32)])
        (up_sum,) = grad_sum("up", s_up, k_up, [(ff, f32)])
        grad_mid, pre_part, attn_part, kv_own, kv_send, grad_q, q_part, s_out, k_out = call(
            attn_grad_body,
            [wide_f, ((1, width), f32), ((1, width), f32), ((t, hd), f32), ((t, hd), f32),
             ((t, qw), bf16), ((1, hd), f32)] + first_shapes("out", qw),
            part, swap_col(send), mid, proj, cotangent, gains, *wo, q, k, v, probs,
            raw_q, cos, sin, gq, heads, scalars=sc,
            scratch=[pltpu.VMEM((width, qw), bf16), pltpu.VMEM((2, half_width, qw), f32)],
        )
        (out_sum,) = grad_sum("out", s_out, k_out, [(qw, f32)])
        n_qkv = joint_width + gain_cols
        s_qkv, k_qkv, part, send = call(
            joint_body, first_shapes("qkv", n_qkv) + [wide_f, wide_b],
            kv_own, swap_col(kv_send), kv_mine, cos, sin, gk, grad_q, normed,
            x, attn_part, pre_part, post_part, q_part, *w_joint, scalars=sc,
            scratch=[pltpu.VMEM((width, joint_width), bf16),
                     pltpu.VMEM((2, half_width, n_qkv), f32)],
        )
        query_sum, kv_sum = grad_sum(
            "qkv", s_qkv, k_qkv, [(qw, f32), (hd + gain_cols, bf16)]
        )
        in_own_t, in_send = call(
            input_body, out_pair,
            part, swap_col(send), x, grad_mid, gains,
        )
        both = diag_to_off_row(jnp.concatenate([out_send, in_send], axis=0)).astype(f32)
        block_output = jnp.where(diag, out_own_t, both[:half_width]).T
        input_grad = jnp.where(diag, in_own_t, both[half_width:]).T
        key_sum, value_sum, gain_sum = call(
            finish_body,
            [((half_width, hd), f32), ((half_width, hd), f32), ((8, half_width), f32)],
            kv_sum, swap_col(kv_sum), scalars=sc, out_hbm=2,
        )
        return (
            block_output, input_grad, query_sum, key_sum, value_sum, out_sum.T,
            gate_sum, up_sum, down_sum.T,
            gain_sum[0], gain_sum[1], gain_sum[2], gain_sum[3],
            gain_sum[4, :hd], gain_sum[5, :hd],
        )

    return step


def solution(mesh):
    rows_by_width = P(("dp", "col"), "row")
    in_specs = (
        rows_by_width, P(("dp", "row"), None), P("row", "col"), P("row", None), P("row", None),
        P("col", "row"), P("row", "col"), P("row", "col"), P("col", "row"),
        P("row"), P("row"), P("row"), P("row"), P(), P(), rows_by_width,
    )
    out_specs = (
        rows_by_width, rows_by_width, P("row", "col"), P("row", None), P("row", None),
        P("col", "row"), P("row", "col"), P("row", "col"), P("col", "row"),
        P("row"), P("row"), P("row"), P("row"), P(), P(),
    )
    return jax.shard_map(
        make_step(mesh), mesh=mesh, in_specs=in_specs, out_specs=out_specs, check_vma=False
    )
```
